128 devices in a mesh: row: 16 (over y, x_hi, core), col: 8 (over x_lo, z).
Axes of the slice: x: 4 (x_hi: 2, x_lo: 2; x = x_hi * 2 + x_lo), y: 4, z: 4, core: 2. Of those that a mesh axis runs over, the one named last changes fastest.
Arguments:
- field: bfloat16 [128, 128, 512], P('row', 'col'), may hold values from -6 to 6
- in_weight: bfloat16 [512, 2048], P(None, 'row'), may hold values from -0.25 to 0.25
- conv_weight: float32 [3, 3, 1024], replicated, may hold values from -2 to 2
- proj_weight: bfloat16 [1024, 256], replicated, may hold values from -0.1875 to 0.1875
- dt_weight: bfloat16 [4, 32, 1024], replicated, may hold values from -1 to 1
- dt_bias: float32 [4, 1024], replicated, may hold values from -7 to -2
- decay_rate: float32 [4, 16, 1024], replicated, may hold values from 0.5 to 2
- skip_gain: float32 [4, 1024], replicated, may hold values from 0.1 to 1.9
- norm_gain: float32 [1024], replicated, may hold values from 0.1 to 1.9
- out_weight: bfloat16 [1024, 512], P('col'), may hold values from -0.1875 to 0.1875
- grad_out: bfloat16 [128, 128, 512], P('row', 'col'), may hold values from -6 to 6
Outputs:
- result: bfloat16 [128, 128, 512], P('row', 'col')
- grad_field: float32 [128, 128, 512], P('row', 'col')
- grad_in_weight: float32 [512, 2048], P(None, 'row')
- grad_out_weight: float32 [1024, 512], P('col')
The draws below stay inside these ranges and needn't reach their ends.
All inputs are finite; a program needn't handle non-finite values.
Results may differ from the reference program's by a relative error of at most 0.0073.
Values may be sent and summed in bfloat16 or wider, within the bound.
No kernel may reach another device: no remote copies, remote signals or barrier semaphores. Data moves between devices by JAX's collectives and lax.ppermute only.
A program may use at most 256 MiB of HBM per device.

```python
import math
import jax
import jax.numpy as jnp
from jax import lax

C = 512
E = 1024
N = 16
R = 32
K = 4
H = 128
W = 128


def draw_dt_bias(key, part):
    return jax.random.uniform(key, (K, E), jnp.float32, -6.0, -2.0)


def steps_of(own_key, extent, split, least, top_value):
    def one(position, blocks):
        draws = jax.random.uniform(jax.random.fold_in(jax.random.fold_in(own_key, 6), position), (blocks,), jnp.float32, least / len(split), top_value / len(split))
        return jnp.repeat(jnp.exp(draws), extent[position] // blocks).reshape((-1,) + (1,) * (len(extent) - position - 1))

    factor_of = one(*split[0])
    for cut in split[1:]:
        factor_of = factor_of * one(*cut)
    return factor_of


def scatter_about(key, shape, deviation, limit, split=(), dtype=jnp.bfloat16):
    values = jax.random.normal(key, shape, jnp.float32) * deviation
    if len(split) > 0:
        values = steps_of(key, shape, split, -0.22, 0.18) * values
    return jnp.clip(values, min=-limit, max=limit).astype(dtype)


def setup_inputs(seed: int = 0) -> dict:
    key_list = jax.random.split(jax.random.key(seed), 12)
    field = scatter_about(key_list[0], (H, W, C), 1.0, 6.0, ((0, 16), (1, 8)))
    in_weight = scatter_about(key_list[1], (C, 2 * E), C ** -0.5, 0.25, ((1, 16),))
    conv_weight = scatter_about(key_list[2], (3, 3, E), 9 ** -0.5, 2.0, (), jnp.float32)
    proj_weight = scatter_about(key_list[3], (E, K * (R + 2 * N)), E ** -0.5, 0.1875)
    dt_weight = scatter_about(key_list[4], (K, R, E), R ** -0.5, 1.0)
    dt_bias = draw_dt_bias(jax.random.fold_in(key_list[11], 71), 0)
    decay_rate = jnp.clip(jnp.exp(jax.random.uniform(key_list[6], (K, N, E), jnp.float32, math.log(0.5), math.log(2.0))), 0.5, 2.0)
    skip_gain = jnp.clip(1.0 + 0.18 * jax.random.normal(key_list[7], (K, E), jnp.float32), 0.1, 1.9)
    norm_gain = jnp.clip(1.0 + 0.18 * jax.random.normal(key_list[8], (E,), jnp.float32), 0.1, 1.9)
    out_weight = scatter_about(key_list[9], (E, C), E ** -0.5, 0.1875, ((0, 8),))
    grad_out = scatter_about(key_list[10], (H, W, C), 1.0, 6.0, ((0, 16), (1, 8)))
    return {"field": field, "in_weight": in_weight, "conv_weight": conv_weight, "proj_weight": proj_weight, "dt_weight": dt_weight, "dt_bias": dt_bias, "decay_rate": decay_rate, "skip_gain": skip_gain, "norm_gain": norm_gain, "out_weight": out_weight, "grad_out": grad_out}


DT_FLOOR = 0.004
NORM_EPS = 1e-05
TOP_PRECISION = lax.Precision.HIGHEST

def arrange(values, direction):
    if direction >= 2:
        values = jnp.swapaxes(values, 0, 1)
    if direction % 2 == 1:
        values = jnp.flip(values, 0)
    return values

def restore(values, direction):
    if direction % 2 == 1:
        values = jnp.flip(values, 0)
    if direction >= 2:
        values = jnp.swapaxes(values, 0, 1)
    return values

def prepare(projected, dt_matrix, dt_offset):
    rank_part = projected[..., :R]
    step_sizes = DT_FLOOR + jax.nn.softplus(jnp.einsum('plr,re->ple', rank_part, dt_matrix, precision=TOP_PRECISION) + dt_offset)
    return (step_sizes, projected[..., R:R + N], projected[..., R + N:])

def line_sums(inputs, projected, dt_matrix, dt_offset, decay_rates):
    step_sizes, in_coef, _ = prepare(projected, dt_matrix, dt_offset)
    running = jnp.cumsum(step_sizes, axis=0)
    totals = running[-1]
    weights = jnp.exp(-decay_rates * (totals[None, :, None, :] - running[:, :, None, :]))
    driven = (step_sizes * inputs)[:, :, None, :] * in_coef[:, :, :, None]
    return (totals, lax.optimization_barrier(jnp.sum(weights * driven, axis=0)))

def line_outputs(inputs, projected, dt_matrix, dt_offset, decay_rates, skip_row, start_state):
    step_sizes, in_coef, out_coef = prepare(projected, dt_matrix, dt_offset)

    def advance(cell_state, slice_now):
        step_now, input_now, in_now, out_now = slice_now
        cell_state = jnp.exp(-step_now[:, None, :] * decay_rates) * cell_state + (step_now * input_now)[:, None, :] * in_now[:, :, None]
        return (cell_state, jnp.einsum('lne,ln->le', cell_state, out_now, precision=TOP_PRECISION))
    _, outputs = lax.scan(advance, start_state, (step_sizes, inputs, in_coef, out_coef))
    return outputs + skip_row * inputs

def run_lines(inputs, projected, dt_matrix, dt_offset, decay_rates, skip_row):
    line_length = inputs.shape[0]
    line_count = inputs.shape[1]
    block_size = math.gcd(line_count, 8)
    block_count = line_count // block_size

    def solve_block(block_pair):
        part_in, part_proj = block_pair
        totals, end_states = line_sums(part_in, part_proj, dt_matrix, dt_offset, decay_rates)
        start_state = end_states / (1.0 - jnp.exp(-decay_rates * totals[:, None, :]))
        return line_outputs(part_in, part_proj, dt_matrix, dt_offset, decay_rates, skip_row, start_state)
    solve_block = jax.checkpoint(solve_block)
    split_in = inputs.reshape(line_length, block_count, block_size, inputs.shape[2]).transpose(1, 0, 2, 3)
    split_proj = projected.reshape(line_length, block_count, block_size, projected.shape[2]).transpose(1, 0, 2, 3)
    outputs = lax.map(solve_block, (split_in, split_proj))
    return outputs.transpose(1, 0, 2, 3).reshape(line_length, line_count, inputs.shape[2])

def finish(summed, gate_part, norm_gain):
    centre = lax.optimization_barrier(jnp.mean(summed, axis=-1, keepdims=True))
    spread = lax.optimization_barrier(jnp.mean(jnp.square(summed - centre), axis=-1, keepdims=True))
    normed = (summed - centre) * lax.rsqrt(spread + NORM_EPS) * norm_gain
    return normed * jax.nn.silu(gate_part)

def reference(field, in_weight, conv_weight, proj_weight, dt_weight, dt_bias, decay_rate, skip_gain, norm_gain, out_weight, grad_out):
    field_rows = field.reshape(H * W, C)
    mixed_in = jnp.dot(field_rows, in_weight, preferred_element_type=jnp.float32).astype(jnp.bfloat16).reshape(H, W, 2 * E)
    proj_table = proj_weight.astype(jnp.float32)

    def inner_part(source_gate):
        source = source_gate[..., :E]
        gate_part = source_gate[..., E:]
        convolved = jnp.zeros((H, W, E), jnp.float32)
        for row_off in range(3):
            for col_off in range(3):
                convolved = convolved + jnp.roll(source, (1 - row_off, 1 - col_off), axis=(0, 1)) * conv_weight[row_off, col_off]
        active = jax.nn.silu(convolved)
        active = active + lax.stop_gradient(active.astype(jnp.bfloat16).astype(jnp.float32) - active)
        projected = jnp.einsum('hwe,ef->hwf', active, proj_table, precision=TOP_PRECISION).reshape(H, W, K, R + 2 * N)
        summed = jnp.zeros((H, W, E), jnp.float32)
        for direction in range(K):
            lined = run_lines(arrange(active, direction), arrange(projected[:, :, direction, :], direction), dt_weight[direction].astype(jnp.float32), dt_bias[direction], decay_rate[direction], skip_gain[direction])
            summed = summed + restore(lined, direction)
        return finish(summed, gate_part, norm_gain)
    mixed_full, pullback = jax.vjp(inner_part, mixed_in.astype(jnp.float32))
    mixed = mixed_full.astype(jnp.bfloat16).reshape(H * W, E)
    result = (field_rows.astype(jnp.float32) + jnp.dot(mixed, out_weight, preferred_element_type=jnp.float32)).astype(jnp.bfloat16).reshape(H, W, C)
    grad_rows = grad_out.reshape(H * W, C)
    back_mixed = jnp.dot(grad_rows, out_weight.T, preferred_element_type=jnp.float32)
    grad_out_weight = jnp.dot(mixed.T, grad_rows, preferred_element_type=jnp.float32)
    back_xz = pullback(back_mixed.reshape(H, W, E))[0].astype(jnp.bfloat16).reshape(H * W, 2 * E)
    grad_field = (grad_rows.astype(jnp.float32) + jnp.dot(back_xz, in_weight.T, preferred_element_type=jnp.float32)).reshape(H, W, C)
    grad_in_weight = jnp.dot(field_rows.T, back_xz, preferred_element_type=jnp.float32)
    return (result, grad_field, grad_in_weight, grad_out_weight)
```

```python
from functools import partial

import jax
import jax.numpy as jnp
from jax import lax
from jax.experimental import pallas as pl
from jax.experimental.pallas import tpu as pltpu
from jax.sharding import PartitionSpec as P

C = 512
E = 1024
N = 16
R = 32
K = 4
ROWS = 8
COLS = 16
CELLS = ROWS * COLS
LANES = 128
TILES = E // LANES
SLABS = CELLS // 8
WIDE = 512
GROUP = 8
LOG2E = 1.4426950408889634

DT_FLOOR = 0.004
NORM_EPS = 1e-05

F32 = jnp.float32
BF16 = jnp.bfloat16


def slab_rows(down, d, t):
    if down:
        half, p = divmod(t, ROWS)
        row = ROWS - 1 - p if d else p
        return pl.ds(row * COLS + half * 8, 8)
    col = COLS - 1 - t if d else t
    return pl.ds(col, 8, stride=COLS)


def chains(down):
    if down:
        return ((0, ROWS, 0), (ROWS, ROWS, 8))
    return ((0, COLS, 0),)


def split(v):
    high = v.astype(BF16)
    return high, (v - high.astype(F32)).astype(BF16)


def into_slabs(down, d, src, put):
    for t in range(SLABS):
        put(t, src[slab_rows(down, d, t), :])


def make_tables(down, proj_ref, psl_ref, tab_ref, first, count):
    for d in range(2):
        for t in range(SLABS):
            psl_ref[d, t * 8 : t * 8 + 8, :] = proj_ref[slab_rows(down, d, t), :]
        spread = psl_ref[d]
        for j in range(count):
            lane = d * (R + 2 * N) + first + j
            tab_ref[d, j] = jnp.broadcast_to(spread[:, lane : lane + 1], (CELLS, LANES))


def at_slab(t):
    if isinstance(t, int):
        return pl.ds(t * 8, 8)
    return pl.ds(pl.multiple_of(t * 8, 8), 8)


def spread_rates(rate_ref, d, nr_ref):
    for n in range(N):
        nr_ref[n] = jnp.broadcast_to(rate_ref[d, n : n + 1, :], (8, LANES))


def put_states(states, es_ref, out_ref, d, line):
    for n in range(N):
        es_ref[pl.ds(n, 8, stride=N), :] = states[n]
    for l in range(8):
        out_ref[line + l, d * N : (d + 1) * N, :] = es_ref[l * N : (l + 1) * N, :].astype(BF16)


def get_states(src_ref, es_ref, d, line):
    for l in range(8):
        es_ref[l * N : (l + 1) * N, :] = src_ref[line + l, d * N : (d + 1) * N, :].astype(F32)
    return [es_ref[pl.ds(n, 8, stride=N), :] for n in range(N)]


def walk(length, step, carry, backwards=False):
    def body(i, carry):
        for q in range(GROUP):
            at = i * GROUP + q
            carry = step(length - 1 - at if backwards else at, carry)
        return carry

    if length == GROUP:
        return body(0, carry)
    return lax.fori_loop(0, length // GROUP, body, carry)


def tree_sum(parts):
    while len(parts) > 1:
        parts = [sum(parts[i + 1 : i + 2], parts[i]) for i in range(0, len(parts), 2)]
    return parts[0]


def sums_kernel(
    active_ref, proj_ref, dtw_ref, bias_ref, rate_ref,
    ends_ref, step_ref, sig_ref,
    psl_ref, tab_ref, xf_ref, us_ref, nr_ref, es_ref, ts_ref,
    *, down,
):
    @pl.when(pl.program_id(0) == 0)
    def _():
        make_tables(down, proj_ref, psl_ref, tab_ref, R, N)

    xf_ref[...] = active_ref[...].astype(F32)
    for d in range(2):
        high, low = split(psl_ref[d])
        weights = dtw_ref[d]
        v = (
            jnp.dot(high, weights, preferred_element_type=F32)
            + jnp.dot(low, weights, preferred_element_type=F32)
            + bias_ref[d : d + 1, :]
        )
        small = jnp.exp(-jnp.abs(v))
        steps = DT_FLOOR + jnp.maximum(v, 0.0) + jnp.log(1.0 + small)
        step_ref[d] = steps
        sig_ref[d] = jnp.where(v >= 0.0, 1.0, small) / (1.0 + small)

        def put(t, x):
            us_ref[t * 8 : t * 8 + 8, :] = x * step_ref[d, t * 8 : t * 8 + 8, :]

        into_slabs(down, d, xf_ref, put)
        spread_rates(rate_ref, d, nr_ref)
        for first, length, line in chains(down):

            def step(p, carry):
                total, states = carry
                rows = at_slab(first + p)
                st = step_ref[d, rows, :]
                u = us_ref[rows, :]
                states = tuple(
                    jnp.exp2(st * nr_ref[n]) * states[n] + u * tab_ref[d, n, rows, :]
                    for n in range(N)
                )
                return total + st, states

            zero = jnp.zeros((8, LANES), F32)
            total, states = walk(length, step, (zero, (zero,) * N))
            put_states(states, es_ref, ends_ref, d, line)
            high = total.astype(BF16).astype(F32)
            ts_ref[pl.ds(line * 8 + 2 * d, 8, stride=8), :] = high
            ts_ref[pl.ds(line * 8 + 2 * d + 1, 8, stride=8), :] = total - high
    lines = COLS if down else ROWS
    for l in range(lines):
        ends_ref[l, 2 * N : 2 * N + 4, :] = ts_ref[l * 8 : l * 8 + 4, :].astype(BF16)


def outputs_kernel(
    active_ref, proj_ref, step_ref, rate_ref, skip_ref, start_ref,
    y_ref, hs_ref,
    psl_ref, tab_ref, xf_ref, us_ref, ys_ref, nr_ref, es_ref,
    *, down,
):
    @pl.when(pl.program_id(0) == 0)
    def _():
        make_tables(down, proj_ref, psl_ref, tab_ref, R, 2 * N)

    xf_ref[...] = active_ref[...].astype(F32)
    y_ref[...] = xf_ref[...] * skip_ref[...]
    for d in range(2):

        def put(t, x):
            us_ref[t * 8 : t * 8 + 8, :] = x * step_ref[d, t * 8 : t * 8 + 8, :]

        into_slabs(down, d, xf_ref, put)
        spread_rates(rate_ref, d, nr_ref)
        for at, (first, length, line) in enumerate(chains(down)):

            def step(p, states):
                rows = at_slab(first + p)
                st = step_ref[d, rows, :]
                u = us_ref[rows, :]
                kept = at_slab(first + at + p)
                for n in range(N):
                    hs_ref[d, n, kept, :] = states[n]
                states = tuple(
                    jnp.exp2(st * nr_ref[n]) * states[n] + u * tab_ref[d, n, rows, :]
                    for n in range(N)
                )
                parts = [states[n] * tab_ref[d, N + n, rows, :] for n in range(N)]
                ys_ref[rows, :] = tree_sum(parts)
                return states

            states = walk(length, step, tuple(get_states(start_ref, es_ref, d, line)))
            for n in range(N):
                hs_ref[d, n, at_slab(first + at + length), :] = states[n]
        for t in range(SLABS):
            rows = slab_rows(down, d, t)
            y_ref[rows, :] = y_ref[rows, :] + ys_ref[t * 8 : t * 8 + 8, :]


def back_sums_kernel(
    dy_ref, proj_ref, step_ref, rate_ref,
    ends_ref,
    psl_ref, tab_ref, dys_ref, nr_ref, es_ref,
    *, down,
):
    @pl.when(pl.program_id(0) == 0)
    def _():
        make_tables(down, proj_ref, psl_ref, tab_ref, R + N, N)

    for d in range(2):

        def put(t, x):
            dys_ref[t * 8 : t * 8 + 8, :] = x

        into_slabs(down, d, dy_ref, put)
        spread_rates(rate_ref, d, nr_ref)
        for first, length, line in chains(down):

            def step(p, states):
                rows = at_slab(first + p)
                st = step_ref[d, rows, :]
                dy = dys_ref[rows, :]
                return tuple(
                    jnp.exp2(st * nr_ref[n]) * (states[n] + dy * tab_ref[d, n, rows, :])
                    for n in range(N)
                )

            zero = jnp.zeros((8, LANES), F32)
            states = walk(length, step, (zero,) * N, backwards=True)
            put_states(states, es_ref, ends_ref, d, line)


def grads_kernel(
    active_ref, dy_ref, proj_ref, step_ref, sig_ref, rate_ref, skip_ref, dtw_ref, hs_ref, tail_ref,
    dx_ref, pg_ref,
    psl_ref, tab_ref, acc_ref, rank_ref, xf_ref, xs_ref, dys_ref, us_ref, dxs_ref, dvs_ref, nr_ref, es_ref,
    *, down,
):
    tile = pl.program_id(0)

    @pl.when(tile == 0)
    def _():
        make_tables(down, proj_ref, psl_ref, tab_ref, R, 2 * N)
        acc_ref[...] = jnp.zeros(acc_ref.shape, F32)
        rank_ref[...] = jnp.zeros(rank_ref.shape, F32)

    xf_ref[...] = active_ref[...].astype(F32)
    dx_ref[...] = dy_ref[...] * skip_ref[...]
    for d in range(2):

        def put(t, x):
            rows = slice(t * 8, t * 8 + 8)
            xs_ref[rows, :] = x
            us_ref[rows, :] = x * step_ref[d, rows, :]

        def put_dy(t, x):
            dys_ref[t * 8 : t * 8 + 8, :] = x

        into_slabs(down, d, xf_ref, put)
        into_slabs(down, d, dy_ref, put_dy)
        spread_rates(rate_ref, d, nr_ref)
        for at, (first, length, line) in enumerate(chains(down)):

            def backward(p, pulls):
                rows = at_slab(first + p)
                before = at_slab(first + at + p)
                after = at_slab(first + at + p + 1)
                st = step_ref[d, rows, :]
                u = us_ref[rows, :]
                dy = dys_ref[rows, :]
                back_u = []
                back_step = []
                new = []
                for n in range(N):
                    acc_ref[d, N + n, rows, :] += hs_ref[d, n, after, :] * dy
                    g = pulls[n] + dy * tab_ref[d, N + n, rows, :]
                    acc_ref[d, n, rows, :] += g * u
                    back_u.append(g * tab_ref[d, n, rows, :])
                    nr = nr_ref[n]
                    ag = jnp.exp2(st * nr) * g
                    back_step.append(ag * hs_ref[d, n, before, :] * nr)
                    new.append(ag)
                    if n % 4 == 3:
                        back_u = [tree_sum(back_u)]
                        back_step = [tree_sum(back_step)]
                back_u = back_u[0]
                dxs_ref[rows, :] = back_u * st
                dvs_ref[rows, :] = (back_step[0] * (1.0 / LOG2E) + back_u * xs_ref[rows, :]) * sig_ref[
                    d, rows, :
                ]
                return tuple(new)

            walk(length, backward, tuple(get_states(tail_ref, es_ref, d, line)), backwards=True)
        for t in range(SLABS):
            rows = slab_rows(down, d, t)
            dx_ref[rows, :] = dx_ref[rows, :] + dxs_ref[t * 8 : t * 8 + 8, :]
        high, low = split(dvs_ref[...])
        dims = (((1,), (1,)), ((), ()))
        rank_ref[d] += lax.dot_general(
            high, dtw_ref[d], dims, preferred_element_type=F32
        ) + lax.dot_general(low, dtw_ref[d], dims, preferred_element_type=F32)

    @pl.when(tile == TILES - 1)
    def _():
        for d in range(2):
            total = rank_ref[d]
            ones = jnp.ones((2 * LANES, LANES), BF16)
            column = lax.broadcasted_iota(jnp.int32, (CELLS, LANES), 1)
            for j in range(2 * N):
                lane = d * (R + 2 * N) + R + j
                both = jnp.concatenate(split(acc_ref[d, j]), axis=1)
                row_sums = jnp.dot(both, ones, preferred_element_type=F32)
                total = jnp.where(column == lane, row_sums, total)
            rank_ref[d] = total
            for t in range(SLABS):
                rows = slab_rows(down, d, t)
                piece = rank_ref[d, t * 8 : t * 8 + 8, :]
                pg_ref[rows, :] = pg_ref[rows, :] + piece if d else piece


def close_kernel(info_ref, ends_ref, rate_ref, out_ref, *, peers, flip):
    own = info_ref.shape[0] // peers
    for i in range(own):
        for d in range(2):
            order = [b * own + i for b in range(peers)]
            if (d == 1) != flip:
                order = order[::-1]
            nr = rate_ref[d]

            def total_of(b):
                return (
                    info_ref[b, 2 * N + 2 * d : 2 * N + 2 * d + 1, :].astype(F32)
                    + info_ref[b, 2 * N + 2 * d + 1 : 2 * N + 2 * d + 2, :].astype(F32)
                )

            def advance(state, b):
                end = ends_ref[b, d * N : (d + 1) * N, :].astype(F32)
                return jnp.exp2(nr * total_of(b)) * state + end

            state = jnp.zeros((N, WIDE), F32)
            loop = jnp.zeros((1, WIDE), F32)
            for b in order:
                state = advance(state, b)
                loop = loop + total_of(b)
            state = state / (1.0 - jnp.exp2(nr * loop))
            for b in order:
                out_ref[b, d * N : (d + 1) * N, :] = state.astype(BF16)
                state = advance(state, b)


def tail_kernel(y0_ref, y1_ref, gate_ref, gain_ref, back_ref, mixed_ref, back_sum_ref, back_gate_ref):
    summed = y0_ref[...] + y1_ref[...]
    centred = summed - jnp.mean(summed, axis=-1, keepdims=True)
    spread = jnp.mean(centred * centred, axis=-1, keepdims=True)
    scale = lax.rsqrt(spread + NORM_EPS)
    unit = centred * scale
    gain = gain_ref[...]
    normed = unit * gain
    gate = gate_ref[...].astype(F32)
    sig = 1.0 / (1.0 + jnp.exp(-gate))
    gated = gate * sig
    back = back_ref[...]
    mixed_ref[...] = (normed * gated).astype(BF16)
    back_gate_ref[...] = (back * normed * (sig + gated * (1.0 - sig))).astype(BF16)
    back_unit = back * gated * gain
    back_sum_ref[...] = scale * (
        back_unit
        - jnp.mean(back_unit, axis=-1, keepdims=True)
        - unit * jnp.mean(back_unit * unit, axis=-1, keepdims=True)
    )


def tiled(lead):
    zeros = (0,) * len(lead)
    return pl.BlockSpec((*lead, LANES), lambda i: (*zeros, i))


def by_tile(lead):
    zeros = (0,) * (len(lead) + 1)
    return pl.BlockSpec((None, *lead, LANES), lambda i: (i, *zeros))


def whole(shape):
    zeros = (0,) * len(shape)
    return pl.BlockSpec(shape, lambda i: zeros)


def vmem(*shape):
    return pltpu.VMEM(shape, F32)


PAIR = (2, CELLS)
PARAMS = pltpu.CompilerParams(dimension_semantics=("arbitrary",), vmem_limit_bytes=56 * 1024 * 1024)


def call(kernel, name, specs, outs, scratch, args):
    return pl.pallas_call(
        kernel,
        grid=(TILES,),
        in_specs=specs,
        out_specs=[spec for spec, _ in outs],
        out_shape=[jax.ShapeDtypeStruct(shape, dtype) for _, (shape, dtype) in outs],
        scratch_shapes=scratch,
        compiler_params=PARAMS,
        name=name,
    )(*args)


def block_sums(down, active, proj, dtw, bias, rates):
    lines = COLS if down else ROWS
    return call(
        partial(sums_kernel, down=down),
        "sums_down" if down else "sums_across",
        [tiled((CELLS,)), whole((CELLS, LANES)), tiled((2, LANES)), tiled((2,)), tiled((2, N))],
        [
            (tiled((lines, 2 * N + 4)), ((lines, 2 * N + 4, E), BF16)),
            (by_tile(PAIR), ((TILES, *PAIR, LANES), F32)),
            (by_tile(PAIR), ((TILES, *PAIR, LANES), F32)),
        ],
        [
            vmem(2, CELLS, LANES), vmem(2, N, CELLS, LANES), vmem(CELLS, LANES), vmem(CELLS, LANES),
            vmem(N, 8, LANES), vmem(8 * N, LANES), vmem(lines * 8, LANES),
        ],
        (active, proj, dtw, bias, rates),
    )


def kept_rows(down):
    return CELLS + 8 * len(chains(down))


def block_outputs(down, active, proj, steps, rates, skip, starts):
    lines = COLS if down else ROWS
    return call(
        partial(outputs_kernel, down=down),
        "outputs_down" if down else "outputs_across",
        [
            tiled((CELLS,)), whole((CELLS, LANES)), by_tile(PAIR), tiled((2, N)), tiled((1,)),
            tiled((lines, 2 * N)),
        ],
        [
            (tiled((CELLS,)), ((CELLS, E), F32)),
            (by_tile((2, N, kept_rows(down))), ((TILES, 2, N, kept_rows(down), LANES), F32)),
        ],
        [
            vmem(2, CELLS, LANES), vmem(2, 2 * N, CELLS, LANES), vmem(CELLS, LANES), vmem(CELLS, LANES),
            vmem(CELLS, LANES), vmem(N, 8, LANES), vmem(8 * N, LANES),
        ],
        (active, proj, steps, rates, skip, starts),
    )


def block_back_sums(down, back, proj, steps, rates):
    lines = COLS if down else ROWS
    return call(
        partial(back_sums_kernel, down=down),
        "back_sums_down" if down else "back_sums_across",
        [tiled((CELLS,)), whole((CELLS, LANES)), by_tile(PAIR), tiled((2, N))],
        [(tiled((lines, 2 * N)), ((lines, 2 * N, E), BF16))],
        [
            vmem(2, CELLS, LANES), vmem(2, N, CELLS, LANES), vmem(CELLS, LANES),
            vmem(N, 8, LANES), vmem(8 * N, LANES),
        ],
        (back, proj, steps, rates),
    )[0]


def block_grads(down, active, back, proj, steps, sigs, rates, skip, dtw, kept, tails):
    lines = COLS if down else ROWS
    cells = vmem(CELLS, LANES)
    return call(
        partial(grads_kernel, down=down),
        "grads_down" if down else "grads_across",
        [
            tiled((CELLS,)), tiled((CELLS,)), whole((CELLS, LANES)), by_tile(PAIR), by_tile(PAIR),
            tiled((2, N)), tiled((1,)), tiled((2, LANES)),
            by_tile((2, N, kept_rows(down))), tiled((lines, 2 * N)),
        ],
        [
            (tiled((CELLS,)), ((CELLS, E), F32)),
            (whole((CELLS, LANES)), ((CELLS, LANES), F32)),
        ],
        [
            vmem(2, CELLS, LANES), vmem(2, 2 * N, CELLS, LANES), vmem(2, 2 * N, CELLS, LANES),
            vmem(2, CELLS, LANES), cells, cells, cells, cells, cells, cells,
            vmem(N, 8, LANES), vmem(8 * N, LANES),
        ],
        (active, back, proj, steps, sigs, rates, skip, dtw, kept, tails),
    )


def closed(axis, info, ends, rates, flip):
    peers = lax.axis_size(axis)
    lines = info.shape[0]
    def wide(*lead):
        return pl.BlockSpec((*lead, WIDE), lambda i: (*(0,) * len(lead), i))

    return pl.pallas_call(
        partial(close_kernel, peers=peers, flip=flip),
        grid=(E // WIDE,),
        in_specs=[wide(*info.shape[:2]), wide(*ends.shape[:2]), wide(2, N)],
        out_specs=wide(lines, 2 * N),
        out_shape=jax.ShapeDtypeStruct((lines, 2 * N, E), BF16),
        compiler_params=PARAMS,
        name="close_" + axis,
    )(info, ends, rates)


def tail(y0, y1, gate, gain, back):
    rows = pl.BlockSpec((32, E), lambda i: (i, 0))
    return pl.pallas_call(
        tail_kernel,
        grid=(CELLS // 32,),
        in_specs=[rows, rows, rows, pl.BlockSpec((1, E), lambda i: (0, 0)), rows],
        out_specs=[rows, rows, rows],
        out_shape=[
            jax.ShapeDtypeStruct((CELLS, E), BF16),
            jax.ShapeDtypeStruct((CELLS, E), F32),
            jax.ShapeDtypeStruct((CELLS, E), BF16),
        ],
        compiler_params=PARAMS,
        name="tail",
    )(y0, y1, gate, gain, back)


def swapped(x, axis):
    return lax.all_to_all(x, axis, 0, 0, tiled=True)


def sent_to_all(shard, axis):
    peers = lax.axis_size(axis)
    return swapped(jnp.broadcast_to(shard[None], (peers, *shard.shape)), axis)


def across(shard):
    rows = lax.axis_size("row")
    return lax.ppermute(shard, "row", [(i, (i + rows // 2) % rows) for i in range(rows)])


def from_halves(pieces):
    pieces = pieces.reshape(2, 8, C // 2, LANES)
    return pieces.transpose(0, 2, 1, 3).reshape(C, E)


def owner_order(part):
    return part.astype(BF16).reshape(8, 2, 8, 8, C).transpose(1, 0, 2, 3, 4)


def reduced(pieces):
    pieces = lax.all_to_all(pieces.reshape(128, 8, C), ("row", "col"), 0, 0, tiled=True)
    return jnp.sum(pieces.astype(F32), axis=0)


def with_halo(cells, sides, width):
    for axis, dim in sides:
        count = lax.axis_size(axis)
        head = lax.slice_in_dim(cells, 0, width, axis=dim).astype(BF16)
        tail_part = lax.slice_in_dim(
            cells, cells.shape[dim] - width, cells.shape[dim], axis=dim
        ).astype(BF16)
        before = lax.ppermute(tail_part, axis, [(i, (i + 1) % count) for i in range(count)])
        after = lax.ppermute(head, axis, [((i + 1) % count, i) for i in range(count)])
        cells = jnp.concatenate(
            [before.astype(cells.dtype), cells, after.astype(cells.dtype)], axis=dim
        )
    return cells


def local(
    field,
    in_weight,
    conv_weight,
    proj_weight,
    dt_weight,
    dt_bias,
    decay_rate,
    skip_gain,
    norm_gain,
    out_weight,
    grad_out,
):
    upper = lax.axis_index("row") >= lax.axis_size("row") // 2
    first, last = in_weight[: C // 2], in_weight[C // 2 :]
    other = across(jnp.where(upper, first, last))
    in_source = sent_to_all(jnp.where(upper, other, first), "row")
    in_gate = jnp.where(upper, last, other)
    in_source, in_gate, out_weight = lax.optimization_barrier((in_source, in_gate, out_weight))
    in_source = from_halves(in_source)
    in_gate = from_halves(lax.all_gather(in_gate, "row"))
    out_full = lax.all_gather(out_weight, "col").reshape(E, C)
    field_rows = field.reshape(CELLS, C)
    grad_rows = grad_out.reshape(CELLS, C)
    field_wide = with_halo(field, (("row", 0), ("col", 1)), 1)
    padded = lax.dot_general(
        field_wide, in_source, (((2,), (0,)), ((), ())), preferred_element_type=F32
    ).astype(BF16)
    gate = jnp.dot(field_rows, in_gate, preferred_element_type=F32).astype(BF16)
    convolved = jnp.zeros((ROWS, COLS, E), F32)
    for a in range(3):
        for b in range(3):
            convolved = (
                convolved + padded[a : a + ROWS, b : b + COLS].astype(F32) * conv_weight[a, b]
            )
    convolved = convolved.reshape(CELLS, E)
    active = jax.nn.silu(convolved).astype(BF16)
    projected = jnp.dot(active, proj_weight, preferred_element_type=F32)
    back_mixed = lax.dot_general(
        grad_rows, out_full, (((1,), (1,)), ((), ())), preferred_element_type=F32
    )

    kinds = ((True, "row", 0), (False, "col", 2))
    width = R + 2 * N
    pads = [
        jnp.stack(
            [
                jnp.pad(dt_weight[k + d], ((d * width, LANES - R - d * width), (0, 0)))
                for d in range(2)
            ]
        )
        for _, _, k in kinds
    ]
    projs = [projected[:, k * width : k * width + LANES] for _, _, k in kinds]
    rates = [decay_rate[k : k + 2] * -LOG2E for _, _, k in kinds]
    skips = [skip_gain[k : k + 1] + skip_gain[k + 1 : k + 2] for _, _, k in kinds]

    sums = [
        block_sums(down, active, projs[i], pads[i], dt_bias[k : k + 2], rates[i])
        for i, (down, _, k) in enumerate(kinds)
    ]
    infos = [swapped(sums[i][0], axis) for i, (_, axis, _) in enumerate(kinds)]
    starts = [
        swapped(closed(axis, infos[i], infos[i], rates[i], False), axis)
        for i, (_, axis, _) in enumerate(kinds)
    ]
    outs = [
        block_outputs(down, active, projs[i], sums[i][1], rates[i], skips[i], starts[i])
        for i, (down, _, _) in enumerate(kinds)
    ]
    mixed, back_summed, back_gate = tail(outs[0][0], outs[1][0], gate, norm_gain[None], back_mixed)
    result = (
        field_rows.astype(F32) + jnp.dot(mixed, out_full, preferred_element_type=F32)
    ).astype(BF16)
    out_part = lax.dot_general(
        mixed, grad_rows, (((0,), (0,)), ((), ())), preferred_element_type=F32
    )
    gate_part = lax.dot_general(
        back_gate, field_rows, (((0,), (0,)), ((), ())), preferred_element_type=F32
    )

    back_ends = [
        swapped(block_back_sums(down, back_summed, projs[i], sums[i][1], rates[i]), axis)
        for i, (down, axis, _) in enumerate(kinds)
    ]
    tails = [
        swapped(closed(axis, infos[i], back_ends[i], rates[i], True), axis)
        for i, (_, axis, _) in enumerate(kinds)
    ]
    out_pieces = out_part.astype(BF16).reshape(8, 16, 8, C).transpose(1, 0, 2, 3)
    out_pieces, tails = lax.optimization_barrier((out_pieces, tails))
    out_piece = reduced(out_pieces)
    grads_of = [
        partial(
            block_grads, down, active, back_summed, projs[i], sums[i][1], sums[i][2], rates[i],
            skips[i], pads[i], outs[i][1],
        )
        for i, (down, _, _) in enumerate(kinds)
    ]
    grads = [grads_of[0](tails[0])]
    out_piece, gate_pieces, grads[0], tails[1] = lax.optimization_barrier(
        (out_piece, owner_order(gate_part), grads[0], tails[1])
    )
    gate_piece = reduced(gate_pieces)
    grads.append(grads_of[1](tails[1]))
    out_piece, gate_piece, grads = lax.optimization_barrier((out_piece, gate_piece, grads))
    grad_out_weight = sent_to_all(out_piece, "row").reshape(E // 8, C)
    proj_grads = jnp.concatenate([grads[0][1], grads[1][1]], axis=1)
    high, low = split(proj_grads)
    dims = (((1,), (1,)), ((), ()))
    back_active = (
        grads[0][0]
        + grads[1][0]
        + lax.dot_general(high, proj_weight, dims, preferred_element_type=F32)
        + lax.dot_general(low, proj_weight, dims, preferred_element_type=F32)
    )
    sig = jax.nn.sigmoid(convolved)
    back_conv = back_active * (sig + convolved * sig * (1.0 - sig))
    wide = with_halo(back_conv.reshape(ROWS, COLS, E), (("row", 0), ("col", 1)), 1)
    back_source = jnp.zeros((ROWS, COLS, E), F32)
    for a in range(3):
        for b in range(3):
            back_source = (
                back_source + wide[2 - a : 2 - a + ROWS, 2 - b : 2 - b + COLS] * conv_weight[a, b]
            )
    back_source = back_source.reshape(CELLS, E).astype(BF16)
    source_part = lax.dot_general(
        back_source, field_rows, (((0,), (0,)), ((), ())), preferred_element_type=F32
    )
    source_piece = reduced(owner_order(source_part))
    dims = (((1,), (1,)), ((), ()))
    grad_field = (
        grad_rows.astype(F32)
        + lax.dot_general(back_gate, in_gate, dims, preferred_element_type=F32)
        + lax.dot_general(back_source, in_source, dims, preferred_element_type=F32)
    )
    own = jnp.where(upper, gate_piece, source_piece)
    given = across(jnp.where(upper, source_piece, gate_piece))
    pair = jnp.where(upper, jnp.stack([given, own]), jnp.stack([own, given])).astype(BF16)
    grad_in_weight = (
        sent_to_all(pair, "col").transpose(1, 0, 2, 3).reshape(LANES, C).T.astype(F32)
    )
    return (
        result.reshape(ROWS, COLS, C),
        grad_field.reshape(ROWS, COLS, C),
        grad_in_weight,
        grad_out_weight,
    )


def solution(mesh):
    in_specs = (
        P("row", "col", None),
        P(None, "row"),
        P(),
        P(),
        P(),
        P(),
        P(),
        P(),
        P(),
        P("col", None),
        P("row", "col", None),
    )
    out_specs = (P("row", "col", None), P("row", "col", None), P(None, "row"), P("col", None))
    return jax.shard_map(local, mesh=mesh, in_specs=in_specs, out_specs=out_specs, check_vma=False)
```

```python
from functools import partial

import jax
import jax.numpy as jnp
from jax import lax
from jax.experimental import pallas as pl
from jax.experimental.pallas import tpu as pltpu
from jax.sharding import PartitionSpec as P


C = 512
E = 1024
N = 16
R = 32
ROWS = 8
COLS = 16
CELLS = ROWS * COLS
LANES = 128
TILES = E // LANES
SLABS = CELLS // 8
WIDE = 512
GROUP = 8
LOG2E = 1.4426950408889634

DT_FLOOR = 0.004
NORM_EPS = 1e-05

F32 = jnp.float32
BF16 = jnp.bfloat16


def slab_rows(down, d, t):
    if down:
        half, p = divmod(t, ROWS)
        row = ROWS - 1 - p if d else p
        return pl.ds(row * COLS + half * 8, 8)
    col = COLS - 1 - t if d else t
    return pl.ds(col, 8, stride=COLS)


def chains(down):
    if down:
        return ((0, ROWS, 0), (ROWS, ROWS, 8))
    return ((0, COLS, 0),)


def split(v):
    high = v.astype(BF16)
    return high, (v - high.astype(F32)).astype(BF16)


def into_slabs(down, d, src, put):
    for t in range(SLABS):
        put(t, src[slab_rows(down, d, t), :])


def make_tables(down, proj_ref, psl_ref, tab_ref, first, count):
    for d in range(2):
        for t in range(SLABS):
            psl_ref[d, t * 8 : t * 8 + 8, :] = proj_ref[slab_rows(down, d, t), :]
        spread = psl_ref[d]
        for j in range(count):
            lane = d * (R + 2 * N) + first + j
            tab_ref[d, j] = jnp.broadcast_to(spread[:, lane : lane + 1], (CELLS, LANES))


def at_slab(t):
    if isinstance(t, int):
        return pl.ds(t * 8, 8)
    return pl.ds(pl.multiple_of(t * 8, 8), 8)


def spread_rates(rate_ref, d, nr_ref):
    for n in range(N):
        nr_ref[n] = jnp.broadcast_to(rate_ref[d, n : n + 1, :], (8, LANES))


def put_states(states, es_ref, out_ref, d, line):
    for n in range(N):
        es_ref[pl.ds(n, 8, stride=N), :] = states[n]
    for l in range(8):
        out_ref[line + l, d * N : (d + 1) * N, :] = es_ref[l * N : (l + 1) * N, :].astype(BF16)


def get_states(src_ref, es_ref, d, line):
    for l in range(8):
        es_ref[l * N : (l + 1) * N, :] = src_ref[line + l, d * N : (d + 1) * N, :].astype(F32)
    return [es_ref[pl.ds(n, 8, stride=N), :] for n in range(N)]


def walk(length, step, carry, backwards=False):
    def body(i, carry):
        for q in range(GROUP):
            at = i * GROUP + q
            carry = step(length - 1 - at if backwards else at, carry)
        return carry

    if length == GROUP:
        return body(0, carry)
    return lax.fori_loop(0, length // GROUP, body, carry)


def tree_sum(parts):
    while len(parts) > 1:
        parts = [sum(parts[i + 1 : i + 2], parts[i]) for i in range(0, len(parts), 2)]
    return parts[0]


def sums_kernel(
    active_ref, proj_ref, dtw_ref, bias_ref, rate_ref,
    ends_ref, step_ref, sig_ref,
    psl_ref, tab_ref, xf_ref, us_ref, nr_ref, es_ref, ts_ref,
    *, down,
):
    @pl.when(pl.program_id(0) == 0)
    def _():
        make_tables(down, proj_ref, psl_ref, tab_ref, R, N)

    xf_ref[...] = active_ref[...].astype(F32)
    for d in range(2):
        high, low = split(psl_ref[d])
        weights = dtw_ref[d]
        v = (
            jnp.dot(high, weights, preferred_element_type=F32)
            + jnp.dot(low, weights, preferred_element_type=F32)
            + bias_ref[d : d + 1, :]
        )
        small = jnp.exp(-jnp.abs(v))
        steps = DT_FLOOR + jnp.maximum(v, 0.0) + jnp.log(1.0 + small)
        step_ref[d] = steps
        sig_ref[d] = jnp.where(v >= 0.0, 1.0, small) / (1.0 + small)

        def put(t, x):
            us_ref[t * 8 : t * 8 + 8, :] = x * step_ref[d, t * 8 : t * 8 + 8, :]

        into_slabs(down, d, xf_ref, put)
        spread_rates(rate_ref, d, nr_ref)
        for first, length, line in chains(down):

            def step(p, carry):
                total, states = carry
                rows = at_slab(first + p)
                st = step_ref[d, rows, :]
                u = us_ref[rows, :]
                states = tuple(
                    jnp.exp2(st * nr_ref[n]) * states[n] + u * tab_ref[d, n, rows, :]
                    for n in range(N)
                )
                return total + st, states

            zero = jnp.zeros((8, LANES), F32)
            total, states = walk(length, step, (zero, (zero,) * N))
            put_states(states, es_ref, ends_ref, d, line)
            high = total.astype(BF16).astype(F32)
            ts_ref[pl.ds(line * 8 + 2 * d, 8, stride=8), :] = high
            ts_ref[pl.ds(line * 8 + 2 * d + 1, 8, stride=8), :] = total - high
    lines = COLS if down else ROWS
    for l in range(lines):
        ends_ref[l, 2 * N : 2 * N + 4, :] = ts_ref[l * 8 : l * 8 + 4, :].astype(BF16)


def outputs_kernel(
    active_ref, proj_ref, step_ref, rate_ref, skip_ref, start_ref,
    y_ref, hs_ref,
    psl_ref, tab_ref, xf_ref, us_ref, ys_ref, nr_ref, es_ref,
    *, down,
):
    @pl.when(pl.program_id(0) == 0)
    def _():
        make_tables(down, proj_ref, psl_ref, tab_ref, R, 2 * N)

    xf_ref[...] = active_ref[...].astype(F32)
    y_ref[...] = xf_ref[...] * skip_ref[...]
    for d in range(2):

        def put(t, x):
            us_ref[t * 8 : t * 8 + 8, :] = x * step_ref[d, t * 8 : t * 8 + 8, :]

        into_slabs(down, d, xf_ref, put)
        spread_rates(rate_ref, d, nr_ref)
        for at, (first, length, line) in enumerate(chains(down)):

            def step(p, states):
                rows = at_slab(first + p)
                st = step_ref[d, rows, :]
                u = us_ref[rows, :]
                kept = at_slab(first + at + p)
                for n in range(N):
                    hs_ref[d, n, kept, :] = states[n]
                states = tuple(
                    jnp.exp2(st * nr_ref[n]) * states[n] + u * tab_ref[d, n, rows, :]
                    for n in range(N)
                )
                parts = [states[n] * tab_ref[d, N + n, rows, :] for n in range(N)]
                ys_ref[rows, :] = tree_sum(parts)
                return states

            states = walk(length, step, tuple(get_states(start_ref, es_ref, d, line)))
            for n in range(N):
                hs_ref[d, n, at_slab(first + at + length), :] = states[n]
        for t in range(SLABS):
            rows = slab_rows(down, d, t)
            y_ref[rows, :] = y_ref[rows, :] + ys_ref[t * 8 : t * 8 + 8, :]


def back_sums_kernel(
    dy_ref, proj_ref, step_ref, rate_ref,
    ends_ref,
    psl_ref, tab_ref, dys_ref, nr_ref, es_ref,
    *, down,
):
    @pl.when(pl.program_id(0) == 0)
    def _():
        make_tables(down, proj_ref, psl_ref, tab_ref, R + N, N)

    for d in range(2):

        def put(t, x):
            dys_ref[t * 8 : t * 8 + 8, :] = x

        into_slabs(down, d, dy_ref, put)
        spread_rates(rate_ref, d, nr_ref)
        for first, length, line in chains(down):

            def step(p, states):
                rows = at_slab(first + p)
                st = step_ref[d, rows, :]
                dy = dys_ref[rows, :]
                return tuple(
                    jnp.exp2(st * nr_ref[n]) * (states[n] + dy * tab_ref[d, n, rows, :])
                    for n in range(N)
                )

            zero = jnp.zeros((8, LANES), F32)
            states = walk(length, step, (zero,) * N, backwards=True)
            put_states(states, es_ref, ends_ref, d, line)


def grads_kernel(
    active_ref, dy_ref, proj_ref, step_ref, sig_ref, rate_ref, skip_ref, dtw_ref, hs_ref, tail_ref,
    dx_ref, pg_ref,
    psl_ref, tab_ref, acc_ref, rank_ref, xf_ref, xs_ref, dys_ref, us_ref, dxs_ref, dvs_ref, nr_ref, es_ref,
    *, down,
):
    tile = pl.program_id(0)

    @pl.when(tile == 0)
    def _():
        make_tables(down, proj_ref, psl_ref, tab_ref, R, 2 * N)
        acc_ref[...] = jnp.zeros(acc_ref.shape, F32)
        rank_ref[...] = jnp.zeros(rank_ref.shape, F32)

    xf_ref[...] = active_ref[...].astype(F32)
    dx_ref[...] = dy_ref[...] * skip_ref[...]
    for d in range(2):

        def put(t, x):
            rows = slice(t * 8, t * 8 + 8)
            xs_ref[rows, :] = x
            us_ref[rows, :] = x * step_ref[d, rows, :]

        def put_dy(t, x):
            dys_ref[t * 8 : t * 8 + 8, :] = x

        into_slabs(down, d, xf_ref, put)
        into_slabs(down, d, dy_ref, put_dy)
        spread_rates(rate_ref, d, nr_ref)
        for at, (first, length, line) in enumerate(chains(down)):

            def backward(p, pulls):
                rows = at_slab(first + p)
                before = at_slab(first + at + p)
                st = step_ref[d, rows, :]
                u = us_ref[rows, :]
                dy = dys_ref[rows, :]
                back_u = []
                back_step = []
                new = []
                for n in range(N):
                    g = pulls[n] + dy * tab_ref[d, N + n, rows, :]
                    acc_ref[d, n, rows, :] += g * u
                    back_u.append(g * tab_ref[d, n, rows, :])
                    nr = nr_ref[n]
                    ag = jnp.exp2(st * nr) * g
                    back_step.append(ag * hs_ref[d, n, before, :] * nr)
                    new.append(ag)
                    if n % 4 == 3:
                        back_u = [tree_sum(back_u)]
                        back_step = [tree_sum(back_step)]
                back_u = back_u[0]
                dxs_ref[rows, :] = back_u * st
                dvs_ref[rows, :] = (back_step[0] * (1.0 / LOG2E) + back_u * xs_ref[rows, :]) * sig_ref[
                    d, rows, :
                ]
                return tuple(new)

            walk(length, backward, tuple(get_states(tail_ref, es_ref, d, line)), backwards=True)
        for t in range(SLABS):
            rows = slab_rows(down, d, t)
            dx_ref[rows, :] = dx_ref[rows, :] + dxs_ref[t * 8 : t * 8 + 8, :]
        high, low = split(dvs_ref[...])
        dims = (((1,), (1,)), ((), ()))
        rank_ref[d] += lax.dot_general(
            high, dtw_ref[d], dims, preferred_element_type=F32
        ) + lax.dot_general(low, dtw_ref[d], dims, preferred_element_type=F32)

    @pl.when(tile == TILES - 1)
    def _():
        for d in range(2):
            total = rank_ref[d]
            for n in range(N):
                total = with_row_sums(total, acc_ref[d, n], d * (R + 2 * N) + R + n)
            rank_ref[d] = total
            from_slabs(down, d, rank_ref, pg_ref)


def with_row_sums(total, values, lane):
    ones = jnp.ones((2 * LANES, LANES), BF16)
    column = lax.broadcasted_iota(jnp.int32, (CELLS, LANES), 1)
    sums = jnp.dot(jnp.concatenate(split(values), axis=1), ones, preferred_element_type=F32)
    return jnp.where(column == lane, sums, total)


def from_slabs(down, d, src_ref, out_ref):
    for t in range(SLABS):
        rows = slab_rows(down, d, t)
        piece = src_ref[d, t * 8 : t * 8 + 8, :]
        out_ref[rows, :] = out_ref[rows, :] + piece if d else piece


def out_grads_kernel(dy_ref, hs_ref, pg_ref, dys_ref, acc_ref, total_ref, *, down):
    n = pl.program_id(0)

    @pl.when(n == 0)
    def _():
        for i in range(TILES):
            acc_ref[...] = dy_ref[:, i * LANES : (i + 1) * LANES]
            for d in range(2):
                for t in range(SLABS):
                    dys_ref[d, i, t * 8 : t * 8 + 8, :] = acc_ref[slab_rows(down, d, t), :]
        total_ref[...] = jnp.zeros(total_ref.shape, F32)

    for d in range(2):
        for at, (first, length, _) in enumerate(chains(down)):
            for p in range(length):
                rows = at_slab(first + p)
                after = at_slab(first + at + p + 1)
                acc_ref[rows, :] = tree_sum(
                    [hs_ref[i, d, after, :] * dys_ref[d, i, rows, :] for i in range(TILES)]
                )
        total_ref[d] = with_row_sums(total_ref[d], acc_ref[...], d * (R + 2 * N) + R + N + n)

    @pl.when(n == N - 1)
    def _():
        for d in range(2):
            from_slabs(down, d, total_ref, pg_ref)


def close_kernel(info_ref, ends_ref, rate_ref, out_ref, *, peers, flip):
    own = info_ref.shape[0] // peers
    for i in range(own):
        for d in range(2):
            order = [b * own + i for b in range(peers)]
            if (d == 1) != flip:
                order = order[::-1]
            nr = rate_ref[d]

            def total_of(b):
                return (
                    info_ref[b, 2 * N + 2 * d : 2 * N + 2 * d + 1, :].astype(F32)
                    + info_ref[b, 2 * N + 2 * d + 1 : 2 * N + 2 * d + 2, :].astype(F32)
                )

            def advance(state, b):
                end = ends_ref[b, d * N : (d + 1) * N, :].astype(F32)
                return jnp.exp2(nr * total_of(b)) * state + end

            state = jnp.zeros((N, WIDE), F32)
            loop = jnp.zeros((1, WIDE), F32)
            for b in order:
                state = advance(state, b)
                loop = loop + total_of(b)
            state = state / (1.0 - jnp.exp2(nr * loop))
            for b in order:
                out_ref[b, d * N : (d + 1) * N, :] = state.astype(BF16)
                state = advance(state, b)


def tail_kernel(y0_ref, y1_ref, gate_ref, gain_ref, back_ref, mixed_ref, back_sum_ref, back_gate_ref):
    summed = y0_ref[...] + y1_ref[...]
    centred = summed - jnp.mean(summed, axis=-1, keepdims=True)
    spread = jnp.mean(centred * centred, axis=-1, keepdims=True)
    scale = lax.rsqrt(spread + NORM_EPS)
    unit = centred * scale
    gain = gain_ref[...]
    normed = unit * gain
    gate = gate_ref[...].astype(F32)
    sig = 1.0 / (1.0 + jnp.exp(-gate))
    gated = gate * sig
    back = back_ref[...]
    mixed_ref[...] = (normed * gated).astype(BF16)
    back_gate_ref[...] = (back * normed * (sig + gated * (1.0 - sig))).astype(BF16)
    back_unit = back * gated * gain
    back_sum_ref[...] = scale * (
        back_unit
        - jnp.mean(back_unit, axis=-1, keepdims=True)
        - unit * jnp.mean(back_unit * unit, axis=-1, keepdims=True)
    )


def tiled(lead):
    zeros = (0,) * len(lead)
    return pl.BlockSpec((*lead, LANES), lambda i: (*zeros, i))


def by_tile(lead):
    zeros = (0,) * (len(lead) + 1)
    return pl.BlockSpec((None, *lead, LANES), lambda i: (i, *zeros))


def whole(shape):
    zeros = (0,) * len(shape)
    return pl.BlockSpec(shape, lambda i: zeros)


def vmem(*shape):
    return pltpu.VMEM(shape, F32)


PAIR = (2, CELLS)
PARAMS = pltpu.CompilerParams(dimension_semantics=("arbitrary",), vmem_limit_bytes=56 * 1024 * 1024)


def call(kernel, specs, outs, scratch, args):
    return pl.pallas_call(
        kernel,
        grid=(TILES,),
        in_specs=specs,
        out_specs=[spec for spec, _ in outs],
        out_shape=[jax.ShapeDtypeStruct(shape, dtype) for _, (shape, dtype) in outs],
        scratch_shapes=scratch,
        compiler_params=PARAMS,
    )(*args)


def block_sums(down, active, proj, dtw, bias, rates):
    lines = COLS if down else ROWS
    return call(
        partial(sums_kernel, down=down),
        [tiled((CELLS,)), whole((CELLS, LANES)), tiled((2, LANES)), tiled((2,)), tiled((2, N))],
        [
            (tiled((lines, 2 * N + 4)), ((lines, 2 * N + 4, E), BF16)),
            (by_tile(PAIR), ((TILES, *PAIR, LANES), F32)),
            (by_tile(PAIR), ((TILES, *PAIR, LANES), F32)),
        ],
        [
            vmem(2, CELLS, LANES), vmem(2, N, CELLS, LANES), vmem(CELLS, LANES), vmem(CELLS, LANES),
            vmem(N, 8, LANES), vmem(8 * N, LANES), vmem(lines * 8, LANES),
        ],
        (active, proj, dtw, bias, rates),
    )


def kept_rows(down):
    return CELLS + 8 * len(chains(down))


def block_outputs(down, active, proj, steps, rates, skip, starts):
    lines = COLS if down else ROWS
    return call(
        partial(outputs_kernel, down=down),
        [
            tiled((CELLS,)), whole((CELLS, LANES)), by_tile(PAIR), tiled((2, N)), tiled((1,)),
            tiled((lines, 2 * N)),
        ],
        [
            (tiled((CELLS,)), ((CELLS, E), F32)),
            (by_tile((2, N, kept_rows(down))), ((TILES, 2, N, kept_rows(down), LANES), F32)),
        ],
        [
            vmem(2, CELLS, LANES), vmem(2, 2 * N, CELLS, LANES), vmem(CELLS, LANES), vmem(CELLS, LANES),
            vmem(CELLS, LANES), vmem(N, 8, LANES), vmem(8 * N, LANES),
        ],
        (active, proj, steps, rates, skip, starts),
    )


def block_back_sums(down, back, proj, steps, rates):
    lines = COLS if down else ROWS
    return call(
        partial(back_sums_kernel, down=down),
        [tiled((CELLS,)), whole((CELLS, LANES)), by_tile(PAIR), tiled((2, N))],
        [(tiled((lines, 2 * N)), ((lines, 2 * N, E), BF16))],
        [
            vmem(2, CELLS, LANES), vmem(2, N, CELLS, LANES), vmem(CELLS, LANES),
            vmem(N, 8, LANES), vmem(8 * N, LANES),
        ],
        (back, proj, steps, rates),
    )[0]


def block_grads(down, active, back, proj, steps, sigs, rates, skip, dtw, kept, tails):
    lines = COLS if down else ROWS
    cells = vmem(CELLS, LANES)
    return call(
        partial(grads_kernel, down=down),
        [
            tiled((CELLS,)), tiled((CELLS,)), whole((CELLS, LANES)), by_tile(PAIR), by_tile(PAIR),
            tiled((2, N)), tiled((1,)), tiled((2, LANES)),
            by_tile((2, N, kept_rows(down))), tiled((lines, 2 * N)),
        ],
        [
            (tiled((CELLS,)), ((CELLS, E), F32)),
            (whole((CELLS, LANES)), ((CELLS, LANES), F32)),
        ],
        [
            vmem(2, CELLS, LANES), vmem(2, 2 * N, CELLS, LANES), vmem(2, N, CELLS, LANES),
            vmem(2, CELLS, LANES), cells, cells, cells, cells, cells, cells,
            vmem(N, 8, LANES), vmem(8 * N, LANES),
        ],
        (active, back, proj, steps, sigs, rates, skip, dtw, kept, tails),
    )


def block_out_grads(down, back, kept):
    rows = kept_rows(down)
    return pl.pallas_call(
        partial(out_grads_kernel, down=down),
        grid=(N,),
        in_specs=[
            whole((CELLS, E)),
            pl.BlockSpec((TILES, 2, None, rows, LANES), lambda n: (0, 0, n, 0, 0)),
        ],
        out_specs=whole((CELLS, LANES)),
        out_shape=jax.ShapeDtypeStruct((CELLS, LANES), F32),
        scratch_shapes=[
            vmem(2, TILES, CELLS, LANES), vmem(CELLS, LANES), vmem(2, CELLS, LANES),
        ],
        compiler_params=PARAMS,
        name="out_grads_down" if down else "out_grads_across",
    )(back, kept)


def closed(axis, info, ends, rates, flip):
    peers = lax.axis_size(axis)
    lines = info.shape[0]

    def wide(*lead):
        return pl.BlockSpec((*lead, WIDE), lambda i: (*(0,) * len(lead), i))

    return pl.pallas_call(
        partial(close_kernel, peers=peers, flip=flip),
        grid=(E // WIDE,),
        in_specs=[wide(*info.shape[:2]), wide(*ends.shape[:2]), wide(2, N)],
        out_specs=wide(lines, 2 * N),
        out_shape=jax.ShapeDtypeStruct((lines, 2 * N, E), BF16),
        compiler_params=PARAMS,
    )(info, ends, rates)


def tail(y0, y1, gate, gain, back):
    rows = pl.BlockSpec((32, E), lambda i: (i, 0))
    return pl.pallas_call(
        tail_kernel,
        grid=(CELLS // 32,),
        in_specs=[rows, rows, rows, pl.BlockSpec((1, E), lambda i: (0, 0)), rows],
        out_specs=[rows, rows, rows],
        out_shape=[
            jax.ShapeDtypeStruct((CELLS, E), BF16),
            jax.ShapeDtypeStruct((CELLS, E), F32),
            jax.ShapeDtypeStruct((CELLS, E), BF16),
        ],
        compiler_params=PARAMS,
        name="tail",
    )(y0, y1, gate, gain, back)


def swap(x, axis):
    return lax.all_to_all(x, axis, 0, 0, tiled=True)


def sent_to_all(shard, axis):
    peers = lax.axis_size(axis)
    return swap(jnp.broadcast_to(shard[None], (peers, *shard.shape)), axis)


def across(shard):
    rows = lax.axis_size("row")
    return lax.ppermute(shard, "row", [(i, (i + rows // 2) % rows) for i in range(rows)])


def from_halves(pieces):
    pieces = pieces.reshape(2, 8, C // 2, LANES)
    return pieces.transpose(0, 2, 1, 3).reshape(C, E)


def owner_order(part):
    return part.astype(BF16).reshape(8, 2, 8, 8, C).transpose(1, 0, 2, 3, 4)


def reduced(pieces, rows):
    pieces = lax.all_to_all(pieces.reshape(128, rows, C), ("row", "col"), 0, 0, tiled=True)
    return jnp.sum(pieces.astype(F32), axis=0)


def with_halo(cells, sides, width):
    for axis, dim in sides:
        count = lax.axis_size(axis)
        head = lax.slice_in_dim(cells, 0, width, axis=dim).astype(BF16)
        tail_part = lax.slice_in_dim(
            cells, cells.shape[dim] - width, cells.shape[dim], axis=dim
        ).astype(BF16)
        before = lax.ppermute(tail_part, axis, [(i, (i + 1) % count) for i in range(count)])
        after = lax.ppermute(head, axis, [((i + 1) % count, i) for i in range(count)])
        cells = jnp.concatenate(
            [before.astype(cells.dtype), cells, after.astype(cells.dtype)], axis=dim
        )
    return cells


def block(
    field,
    in_weight,
    conv_weight,
    proj_weight,
    dt_weight,
    dt_bias,
    decay_rate,
    skip_gain,
    norm_gain,
    out_weight,
    grad_out,
):
    upper = lax.axis_index("row") >= lax.axis_size("row") // 2
    out_full = lax.all_gather(out_weight, "col").reshape(E, C)
    first, last = in_weight[: C // 2], in_weight[C // 2 :]
    other = across(jnp.where(upper, first, last))
    in_source = sent_to_all(jnp.where(upper, other, first), "row")
    in_gate = jnp.where(upper, last, other)
    in_source, in_gate = lax.optimization_barrier((in_source, in_gate))
    in_source = from_halves(in_source)
    in_gate = from_halves(lax.all_gather(in_gate, "row"))
    field_rows = field.reshape(CELLS, C)
    grad_rows = grad_out.reshape(CELLS, C)
    field_wide = with_halo(field, (("row", 0), ("col", 1)), 1)
    padded = lax.dot_general(
        field_wide, in_source, (((2,), (0,)), ((), ())), preferred_element_type=F32
    ).astype(BF16)
    gate = jnp.dot(field_rows, in_gate, preferred_element_type=F32).astype(BF16)
    convolved = jnp.zeros((ROWS, COLS, E), F32)
    for a in range(3):
        for b in range(3):
            convolved = (
                convolved + padded[a : a + ROWS, b : b + COLS].astype(F32) * conv_weight[a, b]
            )
    convolved = convolved.reshape(CELLS, E)
    active = jax.nn.silu(convolved).astype(BF16)
    projected = jnp.dot(active, proj_weight, preferred_element_type=F32)
    back_mixed = lax.dot_general(
        grad_rows, out_full, (((1,), (1,)), ((), ())), preferred_element_type=F32
    )

    kinds = ((True, "row", 0), (False, "col", 2))
    width = R + 2 * N
    pads = [
        jnp.stack(
            [
                jnp.pad(dt_weight[k + d], ((d * width, LANES - R - d * width), (0, 0)))
                for d in range(2)
            ]
        )
        for _, _, k in kinds
    ]
    projs = [projected[:, k * width : k * width + LANES] for _, _, k in kinds]
    rates = [decay_rate[k : k + 2] * -LOG2E for _, _, k in kinds]
    skips = [skip_gain[k : k + 1] + skip_gain[k + 1 : k + 2] for _, _, k in kinds]

    sums = [
        block_sums(down, active, projs[i], pads[i], dt_bias[k : k + 2], rates[i])
        for i, (down, _, k) in enumerate(kinds)
    ]
    infos = [swap(sums[i][0], axis) for i, (_, axis, _) in enumerate(kinds)]
    starts = [
        swap(closed(axis, infos[i], infos[i], rates[i], False), axis)
        for i, (_, axis, _) in enumerate(kinds)
    ]
    outs = [
        block_outputs(down, active, projs[i], sums[i][1], rates[i], skips[i], starts[i])
        for i, (down, _, _) in enumerate(kinds)
    ]
    mixed, back_summed, back_gate = tail(outs[0][0], outs[1][0], gate, norm_gain[None], back_mixed)
    result = (
        field_rows.astype(F32) + jnp.dot(mixed, out_full, preferred_element_type=F32)
    ).astype(BF16)
    out_part = lax.dot_general(
        mixed, grad_rows, (((0,), (0,)), ((), ())), preferred_element_type=F32
    )
    gate_part = lax.dot_general(
        back_gate, field_rows, (((0,), (0,)), ((), ())), preferred_element_type=F32
    )

    back_ends = [
        swap(block_back_sums(down, back_summed, projs[i], sums[i][1], rates[i]), axis)
        for i, (down, axis, _) in enumerate(kinds)
    ]
    pieces = jnp.concatenate(
        [
            out_part.astype(BF16).reshape(8, 16, 8, C).transpose(1, 0, 2, 3).reshape(128, 8, C),
            owner_order(gate_part).reshape(128, 8, C),
        ],
        axis=1,
    )
    out_grads = [
        block_out_grads(down, back_summed, outs[i][1]) for i, (down, _, _) in enumerate(kinds)
    ]
    tails = [
        swap(closed(axis, infos[i], back_ends[i], rates[i], True), axis)
        for i, (_, axis, _) in enumerate(kinds)
    ]
    pieces, tails = lax.optimization_barrier((pieces, tails))
    done_piece = reduced(pieces, 16)
    grads = [
        block_grads(
            down, active, back_summed, projs[i], sums[i][1], sums[i][2], rates[i], skips[i],
            pads[i], outs[i][1], tails[i],
        )
        for i, (down, _, _) in enumerate(kinds)
    ]
    done_piece, grads = lax.optimization_barrier((done_piece, grads))
    grad_out_weight = lax.all_gather(jnp.pad(done_piece[:8], ((0, 56), (0, 0))), "row")
    grad_out_weight = grad_out_weight[:, :8].reshape(E // 8, C)
    gate_piece = done_piece[8:]
    proj_grads = jnp.concatenate([grads[i][1] + out_grads[i] for i in range(2)], axis=1)
    high, low = split(proj_grads)
    dims = (((1,), (1,)), ((), ()))
    back_active = (
        grads[0][0]
        + grads[1][0]
        + lax.dot_general(high, proj_weight, dims, preferred_element_type=F32)
        + lax.dot_general(low, proj_weight, dims, preferred_element_type=F32)
    )
    sig = jax.nn.sigmoid(convolved)
    back_conv = back_active * (sig + convolved * sig * (1.0 - sig))
    wide = with_halo(back_conv.reshape(ROWS, COLS, E), (("row", 0), ("col", 1)), 1)
    back_source = jnp.zeros((ROWS, COLS, E), F32)
    for a in range(3):
        for b in range(3):
            back_source = (
                back_source + wide[2 - a : 2 - a + ROWS, 2 - b : 2 - b + COLS] * conv_weight[a, b]
            )
    back_source = back_source.reshape(CELLS, E).astype(BF16)
    source_part = lax.dot_general(
        back_source, field_rows, (((0,), (0,)), ((), ())), preferred_element_type=F32
    )
    source_piece = reduced(owner_order(source_part).reshape(128, 8, C), 8)
    dims = (((1,), (1,)), ((), ()))
    grad_field = (
        grad_rows.astype(F32)
        + lax.dot_general(back_gate, in_gate, dims, preferred_element_type=F32)
        + lax.dot_general(back_source, in_source, dims, preferred_element_type=F32)
    )
    own = jnp.where(upper, gate_piece, source_piece)
    given = across(jnp.where(upper, source_piece, gate_piece))
    pair = jnp.where(upper, jnp.stack([given, own]), jnp.stack([own, given])).astype(BF16)
    grad_in_weight = (
        sent_to_all(pair, "col").transpose(1, 0, 2, 3).reshape(LANES, C).T.astype(F32)
    )
    return (
        result.reshape(ROWS, COLS, C),
        grad_field.reshape(ROWS, COLS, C),
        grad_in_weight,
        grad_out_weight,
    )


def solution(mesh):
    in_specs = (
        P("row", "col", None),
        P(None, "row"),
        P(),
        P(),
        P(),
        P(),
        P(),
        P(),
        P(),
        P("col", None),
        P("row", "col", None),
    )
    out_specs = (P("row", "col", None), P("row", "col", None), P(None, "row"), P("col", None))
    return jax.shard_map(block, mesh=mesh, in_specs=in_specs, out_specs=out_specs, check_vma=False)
```

```python
from functools import partial

import jax
import jax.numpy as jnp
from jax import lax
from jax.experimental import pallas as pl
from jax.experimental.pallas import tpu as pltpu
from jax.sharding import PartitionSpec as P


C = 512
E = 1024
N = 16
R = 32
ROWS = 8
COLS = 16
CELLS = ROWS * COLS
LANES = 128
TILES = E // LANES
SLABS = CELLS // 8
WIDE = 512
GROUP = 8
LOG2E = 1.4426950408889634

DT_FLOOR = 0.004
NORM_EPS = 1e-05

F32 = jnp.float32
BF16 = jnp.bfloat16


def slab_rows(down, d, t):
    if down:
        half, p = divmod(t, ROWS)
        row = ROWS - 1 - p if d else p
        return pl.ds(row * COLS + half * 8, 8)
    col = COLS - 1 - t if d else t
    return pl.ds(col, 8, stride=COLS)


def chains(down):
    if down:
        return ((0, ROWS, 0), (ROWS, ROWS, 8))
    return ((0, COLS, 0),)


def split(v):
    high = v.astype(BF16)
    return high, (v - high.astype(F32)).astype(BF16)


def into_slabs(down, d, src, put):
    for t in range(SLABS):
        put(t, src[slab_rows(down, d, t), :])


def make_tables(down, proj_ref, psl_ref, tab_ref, first, count):
    for d in range(2):
        for t in range(SLABS):
            psl_ref[d, t * 8 : t * 8 + 8, :] = proj_ref[slab_rows(down, d, t), :]
        spread = psl_ref[d]
        for j in range(count):
            lane = d * (R + 2 * N) + first + j
            tab_ref[d, j] = jnp.broadcast_to(spread[:, lane : lane + 1], (CELLS, LANES))


def at_slab(t):
    if isinstance(t, int):
        return pl.ds(t * 8, 8)
    return pl.ds(pl.multiple_of(t * 8, 8), 8)


def spread_rates(rate_ref, d, nr_ref):
    for n in range(N):
        nr_ref[n] = jnp.broadcast_to(rate_ref[d, n : n + 1, :], (8, LANES))


def put_states(states, es_ref, out_ref, d, line):
    for n in range(N):
        es_ref[pl.ds(n, 8, stride=N), :] = states[n]
    for l in range(8):
        out_ref[line + l, d * N : (d + 1) * N, :] = es_ref[l * N : (l + 1) * N, :].astype(BF16)


def get_states(src_ref, es_ref, d, line):
    for l in range(8):
        es_ref[l * N : (l + 1) * N, :] = src_ref[line + l, d * N : (d + 1) * N, :].astype(F32)
    return [es_ref[pl.ds(n, 8, stride=N), :] for n in range(N)]


def walk(length, step, carry, backwards=False):
    def body(i, carry):
        for q in range(GROUP):
            at = i * GROUP + q
            carry = step(length - 1 - at if backwards else at, carry)
        return carry

    if length == GROUP:
        return body(0, carry)
    return lax.fori_loop(0, length // GROUP, body, carry)


def tree_sum(parts):
    while len(parts) > 1:
        parts = [sum(parts[i + 1 : i + 2], parts[i]) for i in range(0, len(parts), 2)]
    return parts[0]


def sums_kernel(
    active_ref, proj_ref, dtw_ref, bias_ref, rate_ref,
    ends_ref, step_ref, sig_ref,
    psl_ref, tab_ref, xf_ref, us_ref, nr_ref, es_ref, ts_ref,
    *, down,
):
    @pl.when(pl.program_id(0) == 0)
    def _():
        make_tables(down, proj_ref, psl_ref, tab_ref, R, N)

    xf_ref[...] = active_ref[...].astype(F32)
    for d in range(2):
        high, low = split(psl_ref[d])
        weights = dtw_ref[d]
        v = (
            jnp.dot(high, weights, preferred_element_type=F32)
            + jnp.dot(low, weights, preferred_element_type=F32)
            + bias_ref[d : d + 1, :]
        )
        small = jnp.exp(-jnp.abs(v))
        steps = DT_FLOOR + jnp.maximum(v, 0.0) + jnp.log(1.0 + small)
        step_ref[d] = steps
        sig_ref[d] = jnp.where(v >= 0.0, 1.0, small) / (1.0 + small)

        def put(t, x):
            us_ref[t * 8 : t * 8 + 8, :] = x * step_ref[d, t * 8 : t * 8 + 8, :]

        into_slabs(down, d, xf_ref, put)
        spread_rates(rate_ref, d, nr_ref)
        for first, length, line in chains(down):

            def step(p, carry):
                total, states = carry
                rows = at_slab(first + p)
                st = step_ref[d, rows, :]
                u = us_ref[rows, :]
                states = tuple(
                    jnp.exp2(st * nr_ref[n]) * states[n] + u * tab_ref[d, n, rows, :]
                    for n in range(N)
                )
                return total + st, states

            zero = jnp.zeros((8, LANES), F32)
            total, states = walk(length, step, (zero, (zero,) * N))
            put_states(states, es_ref, ends_ref, d, line)
            high = total.astype(BF16).astype(F32)
            ts_ref[pl.ds(line * 8 + 2 * d, 8, stride=8), :] = high
            ts_ref[pl.ds(line * 8 + 2 * d + 1, 8, stride=8), :] = total - high
    lines = COLS if down else ROWS
    for l in range(lines):
        ends_ref[l, 2 * N : 2 * N + 4, :] = ts_ref[l * 8 : l * 8 + 4, :].astype(BF16)


def outputs_kernel(
    active_ref, proj_ref, step_ref, rate_ref, skip_ref, start_ref,
    y_ref, hs_ref,
    psl_ref, tab_ref, xf_ref, us_ref, ys_ref, nr_ref, es_ref,
    *, down,
):
    @pl.when(pl.program_id(0) == 0)
    def _():
        make_tables(down, proj_ref, psl_ref, tab_ref, R, 2 * N)

    xf_ref[...] = active_ref[...].astype(F32)
    y_ref[...] = xf_ref[...] * skip_ref[...]
    for d in range(2):

        def put(t, x):
            us_ref[t * 8 : t * 8 + 8, :] = x * step_ref[d, t * 8 : t * 8 + 8, :]

        into_slabs(down, d, xf_ref, put)
        spread_rates(rate_ref, d, nr_ref)
        for at, (first, length, line) in enumerate(chains(down)):

            def step(p, states):
                rows = at_slab(first + p)
                st = step_ref[d, rows, :]
                u = us_ref[rows, :]
                kept = at_slab(first + at + p)
                for n in range(N):
                    hs_ref[d, n, kept, :] = states[n]
                states = tuple(
                    jnp.exp2(st * nr_ref[n]) * states[n] + u * tab_ref[d, n, rows, :]
                    for n in range(N)
                )
                parts = [states[n] * tab_ref[d, N + n, rows, :] for n in range(N)]
                ys_ref[rows, :] = tree_sum(parts)
                return states

            states = walk(length, step, tuple(get_states(start_ref, es_ref, d, line)))
            for n in range(N):
                hs_ref[d, n, at_slab(first + at + length), :] = states[n]
        for t in range(SLABS):
            rows = slab_rows(down, d, t)
            y_ref[rows, :] = y_ref[rows, :] + ys_ref[t * 8 : t * 8 + 8, :]


def back_sums_kernel(
    dy_ref, proj_ref, step_ref, rate_ref,
    ends_ref,
    psl_ref, tab_ref, dys_ref, nr_ref, es_ref,
    *, down,
):
    @pl.when(pl.program_id(0) == 0)
    def _():
        make_tables(down, proj_ref, psl_ref, tab_ref, R + N, N)

    for d in range(2):

        def put(t, x):
            dys_ref[t * 8 : t * 8 + 8, :] = x

        into_slabs(down, d, dy_ref, put)
        spread_rates(rate_ref, d, nr_ref)
        for first, length, line in chains(down):

            def step(p, states):
                rows = at_slab(first + p)
                st = step_ref[d, rows, :]
                dy = dys_ref[rows, :]
                return tuple(
                    jnp.exp2(st * nr_ref[n]) * (states[n] + dy * tab_ref[d, n, rows, :])
                    for n in range(N)
                )

            zero = jnp.zeros((8, LANES), F32)
            states = walk(length, step, (zero,) * N, backwards=True)
            put_states(states, es_ref, ends_ref, d, line)


def grads_kernel(
    active_ref, dy_ref, proj_ref, step_ref, sig_ref, rate_ref, skip_ref, dtw_ref, hs_ref, tail_ref,
    dx_ref, pg_ref,
    psl_ref, tab_ref, acc_ref, rank_ref, xf_ref, xs_ref, dys_ref, us_ref, dxs_ref, dvs_ref, nr_ref, es_ref,
    *, down,
):
    tile = pl.program_id(0)

    @pl.when(tile == 0)
    def _():
        make_tables(down, proj_ref, psl_ref, tab_ref, R, 2 * N)
        acc_ref[...] = jnp.zeros(acc_ref.shape, F32)
        rank_ref[...] = jnp.zeros(rank_ref.shape, F32)

    xf_ref[...] = active_ref[...].astype(F32)
    dx_ref[...] = dy_ref[...] * skip_ref[...]
    for d in range(2):

        def put(t, x):
            rows = slice(t * 8, t * 8 + 8)
            xs_ref[rows, :] = x
            us_ref[rows, :] = x * step_ref[d, rows, :]

        def put_dy(t, x):
            dys_ref[t * 8 : t * 8 + 8, :] = x

        into_slabs(down, d, xf_ref, put)
        into_slabs(down, d, dy_ref, put_dy)
        spread_rates(rate_ref, d, nr_ref)
        for at, (first, length, line) in enumerate(chains(down)):

            def backward(p, pulls):
                rows = at_slab(first + p)
                before = at_slab(first + at + p)
                st = step_ref[d, rows, :]
                u = us_ref[rows, :]
                dy = dys_ref[rows, :]
                back_u = []
                back_step = []
                new = []
                for n in range(N):
                    g = pulls[n] + dy * tab_ref[d, N + n, rows, :]
                    acc_ref[d, n, rows, :] += g * u
                    back_u.append(g * tab_ref[d, n, rows, :])
                    nr = nr_ref[n]
                    ag = jnp.exp2(st * nr) * g
                    back_step.append(ag * hs_ref[d, n, before, :] * nr)
                    new.append(ag)
                    if n % 4 == 3:
                        back_u = [tree_sum(back_u)]
                        back_step = [tree_sum(back_step)]
                back_u = back_u[0]
                dxs_ref[rows, :] = back_u * st
                dvs_ref[rows, :] = (back_step[0] * (1.0 / LOG2E) + back_u * xs_ref[rows, :]) * sig_ref[
                    d, rows, :
                ]
                return tuple(new)

            walk(length, backward, tuple(get_states(tail_ref, es_ref, d, line)), backwards=True)
        for t in range(SLABS):
            rows = slab_rows(down, d, t)
            dx_ref[rows, :] = dx_ref[rows, :] + dxs_ref[t * 8 : t * 8 + 8, :]
        high, low = split(dvs_ref[...])
        dims = (((1,), (1,)), ((), ()))
        rank_ref[d] += lax.dot_general(
            high, dtw_ref[d], dims, preferred_element_type=F32
        ) + lax.dot_general(low, dtw_ref[d], dims, preferred_element_type=F32)

    @pl.when(tile == TILES - 1)
    def _():
        for d in range(2):
            total = rank_ref[d]
            for n in range(N):
                total = with_row_sums(total, acc_ref[d, n], d * (R + 2 * N) + R + n)
            rank_ref[d] = total
            from_slabs(down, d, rank_ref, pg_ref)


def with_row_sums(total, values, lane):
    ones = jnp.ones((2 * LANES, LANES), BF16)
    column = lax.broadcasted_iota(jnp.int32, (CELLS, LANES), 1)
    sums = jnp.dot(jnp.concatenate(split(values), axis=1), ones, preferred_element_type=F32)
    return jnp.where(column == lane, sums, total)


def from_slabs(down, d, src_ref, out_ref):
    for t in range(SLABS):
        rows = slab_rows(down, d, t)
        piece = src_ref[d, t * 8 : t * 8 + 8, :]
        out_ref[rows, :] = out_ref[rows, :] + piece if d else piece


def out_grads_kernel(dy_ref, hs_ref, pg_ref, dys_ref, acc_ref, total_ref, *, down):
    n = pl.program_id(0)

    @pl.when(n == 0)
    def _():
        for i in range(TILES):
            acc_ref[...] = dy_ref[:, i * LANES : (i + 1) * LANES]
            for d in range(2):
                for t in range(SLABS):
                    dys_ref[d, i, t * 8 : t * 8 + 8, :] = acc_ref[slab_rows(down, d, t), :]
        total_ref[...] = jnp.zeros(total_ref.shape, F32)

    for d in range(2):
        for at, (first, length, _) in enumerate(chains(down)):
            for p in range(length):
                rows = at_slab(first + p)
                after = at_slab(first + at + p + 1)
                acc_ref[rows, :] = tree_sum(
                    [hs_ref[i, d, after, :] * dys_ref[d, i, rows, :] for i in range(TILES)]
                )
        total_ref[d] = with_row_sums(total_ref[d], acc_ref[...], d * (R + 2 * N) + R + N + n)

    @pl.when(n == N - 1)
    def _():
        for d in range(2):
            from_slabs(down, d, total_ref, pg_ref)


def close_kernel(info_ref, ends_ref, rate_ref, out_ref, *, peers, flip):
    own = info_ref.shape[0] // peers
    for i in range(own):
        for d in range(2):
            order = [b * own + i for b in range(peers)]
            if (d == 1) != flip:
                order = order[::-1]
            nr = rate_ref[d]

            def total_of(b):
                return (
                    info_ref[b, 2 * N + 2 * d : 2 * N + 2 * d + 1, :].astype(F32)
                    + info_ref[b, 2 * N + 2 * d + 1 : 2 * N + 2 * d + 2, :].astype(F32)
                )

            def advance(state, b):
                end = ends_ref[b, d * N : (d + 1) * N, :].astype(F32)
                return jnp.exp2(nr * total_of(b)) * state + end

            state = jnp.zeros((N, WIDE), F32)
            loop = jnp.zeros((1, WIDE), F32)
            for b in order:
                state = advance(state, b)
                loop = loop + total_of(b)
            state = state / (1.0 - jnp.exp2(nr * loop))
            for b in order:
                out_ref[b, d * N : (d + 1) * N, :] = state.astype(BF16)
                state = advance(state, b)


def tail_kernel(y0_ref, y1_ref, gate_ref, gain_ref, back_ref, mixed_ref, back_sum_ref, back_gate_ref):
    summed = y0_ref[...] + y1_ref[...]
    centred = summed - jnp.mean(summed, axis=-1, keepdims=True)
    spread = jnp.mean(centred * centred, axis=-1, keepdims=True)
    scale = lax.rsqrt(spread + NORM_EPS)
    unit = centred * scale
    gain = gain_ref[...]
    normed = unit * gain
    gate = gate_ref[...].astype(F32)
    sig = 1.0 / (1.0 + jnp.exp(-gate))
    gated = gate * sig
    back = back_ref[...]
    mixed_ref[...] = (normed * gated).astype(BF16)
    back_gate_ref[...] = (back * normed * (sig + gated * (1.0 - sig))).astype(BF16)
    back_unit = back * gated * gain
    back_sum_ref[...] = scale * (
        back_unit
        - jnp.mean(back_unit, axis=-1, keepdims=True)
        - unit * jnp.mean(back_unit * unit, axis=-1, keepdims=True)
    )


def tiled(lead):
    zeros = (0,) * len(lead)
    return pl.BlockSpec((*lead, LANES), lambda i: (*zeros, i))


def by_tile(lead):
    zeros = (0,) * (len(lead) + 1)
    return pl.BlockSpec((None, *lead, LANES), lambda i: (i, *zeros))


def whole(shape):
    zeros = (0,) * len(shape)
    return pl.BlockSpec(shape, lambda i: zeros)


def vmem(*shape):
    return pltpu.VMEM(shape, F32)


PAIR = (2, CELLS)
PARAMS = pltpu.CompilerParams(dimension_semantics=("arbitrary",), vmem_limit_bytes=56 * 1024 * 1024)


def call(kernel, specs, outs, scratch, args):
    return pl.pallas_call(
        kernel,
        grid=(TILES,),
        in_specs=specs,
        out_specs=[spec for spec, _ in outs],
        out_shape=[jax.ShapeDtypeStruct(shape, dtype) for _, (shape, dtype) in outs],
        scratch_shapes=scratch,
        compiler_params=PARAMS,
    )(*args)


def block_sums(down, active, proj, dtw, bias, rates):
    lines = COLS if down else ROWS
    return call(
        partial(sums_kernel, down=down),
        [tiled((CELLS,)), whole((CELLS, LANES)), tiled((2, LANES)), tiled((2,)), tiled((2, N))],
        [
            (tiled((lines, 2 * N + 4)), ((lines, 2 * N + 4, E), BF16)),
            (by_tile(PAIR), ((TILES, *PAIR, LANES), F32)),
            (by_tile(PAIR), ((TILES, *PAIR, LANES), F32)),
        ],
        [
            vmem(2, CELLS, LANES), vmem(2, N, CELLS, LANES), vmem(CELLS, LANES), vmem(CELLS, LANES),
            vmem(N, 8, LANES), vmem(8 * N, LANES), vmem(lines * 8, LANES),
        ],
        (active, proj, dtw, bias, rates),
    )


def kept_rows(down):
    return CELLS + 8 * len(chains(down))


def block_outputs(down, active, proj, steps, rates, skip, starts):
    lines = COLS if down else ROWS
    return call(
        partial(outputs_kernel, down=down),
        [
            tiled((CELLS,)), whole((CELLS, LANES)), by_tile(PAIR), tiled((2, N)), tiled((1,)),
            tiled((lines, 2 * N)),
        ],
        [
            (tiled((CELLS,)), ((CELLS, E), F32)),
            (by_tile((2, N, kept_rows(down))), ((TILES, 2, N, kept_rows(down), LANES), F32)),
        ],
        [
            vmem(2, CELLS, LANES), vmem(2, 2 * N, CELLS, LANES), vmem(CELLS, LANES), vmem(CELLS, LANES),
            vmem(CELLS, LANES), vmem(N, 8, LANES), vmem(8 * N, LANES),
        ],
        (active, proj, steps, rates, skip, starts),
    )


def block_back_sums(down, back, proj, steps, rates):
    lines = COLS if down else ROWS
    return call(
        partial(back_sums_kernel, down=down),
        [tiled((CELLS,)), whole((CELLS, LANES)), by_tile(PAIR), tiled((2, N))],
        [(tiled((lines, 2 * N)), ((lines, 2 * N, E), BF16))],
        [
            vmem(2, CELLS, LANES), vmem(2, N, CELLS, LANES), vmem(CELLS, LANES),
            vmem(N, 8, LANES), vmem(8 * N, LANES),
        ],
        (back, proj, steps, rates),
    )[0]


def block_grads(down, active, back, proj, steps, sigs, rates, skip, dtw, kept, tails):
    lines = COLS if down else ROWS
    cells = vmem(CELLS, LANES)
    return call(
        partial(grads_kernel, down=down),
        [
            tiled((CELLS,)), tiled((CELLS,)), whole((CELLS, LANES)), by_tile(PAIR), by_tile(PAIR),
            tiled((2, N)), tiled((1,)), tiled((2, LANES)),
            by_tile((2, N, kept_rows(down))), tiled((lines, 2 * N)),
        ],
        [
            (tiled((CELLS,)), ((CELLS, E), F32)),
            (whole((CELLS, LANES)), ((CELLS, LANES), F32)),
        ],
        [
            vmem(2, CELLS, LANES), vmem(2, 2 * N, CELLS, LANES), vmem(2, N, CELLS, LANES),
            vmem(2, CELLS, LANES), cells, cells, cells, cells, cells, cells,
            vmem(N, 8, LANES), vmem(8 * N, LANES),
        ],
        (active, back, proj, steps, sigs, rates, skip, dtw, kept, tails),
    )


def block_out_grads(down, back, kept):
    rows = kept_rows(down)
    return pl.pallas_call(
        partial(out_grads_kernel, down=down),
        grid=(N,),
        in_specs=[
            whole((CELLS, E)),
            pl.BlockSpec((TILES, 2, None, rows, LANES), lambda n: (0, 0, n, 0, 0)),
        ],
        out_specs=whole((CELLS, LANES)),
        out_shape=jax.ShapeDtypeStruct((CELLS, LANES), F32),
        scratch_shapes=[
            vmem(2, TILES, CELLS, LANES), vmem(CELLS, LANES), vmem(2, CELLS, LANES),
        ],
        compiler_params=PARAMS,
        name="out_grads_down" if down else "out_grads_across",
    )(back, kept)


def closed(axis, info, ends, rates, flip):
    peers = lax.axis_size(axis)
    lines = info.shape[0]

    def wide(*lead):
        return pl.BlockSpec((*lead, WIDE), lambda i: (*(0,) * len(lead), i))

    return pl.pallas_call(
        partial(close_kernel, peers=peers, flip=flip),
        grid=(E // WIDE,),
        in_specs=[wide(*info.shape[:2]), wide(*ends.shape[:2]), wide(2, N)],
        out_specs=wide(lines, 2 * N),
        out_shape=jax.ShapeDtypeStruct((lines, 2 * N, E), BF16),
        compiler_params=PARAMS,
    )(info, ends, rates)


def tail(y0, y1, gate, gain, back):
    rows = pl.BlockSpec((32, E), lambda i: (i, 0))
    return pl.pallas_call(
        tail_kernel,
        grid=(CELLS // 32,),
        in_specs=[rows, rows, rows, pl.BlockSpec((1, E), lambda i: (0, 0)), rows],
        out_specs=[rows, rows, rows],
        out_shape=[
            jax.ShapeDtypeStruct((CELLS, E), BF16),
            jax.ShapeDtypeStruct((CELLS, E), F32),
            jax.ShapeDtypeStruct((CELLS, E), BF16),
        ],
        compiler_params=PARAMS,
        name="tail",
    )(y0, y1, gate, gain, back)


def swap(x, axis):
    return lax.all_to_all(x, axis, 0, 0, tiled=True)


def sent_to_all(shard, axis):
    peers = lax.axis_size(axis)
    return swap(jnp.broadcast_to(shard[None], (peers, *shard.shape)), axis)


def across(shard):
    rows = lax.axis_size("row")
    return lax.ppermute(shard, "row", [(i, (i + rows // 2) % rows) for i in range(rows)])


def doubled(shard, axis):
    gathered = shard[None]
    for bit in range(lax.axis_size(axis).bit_length() - 1):
        step = 1 << bit
        swaps = [(i, i ^ step) for i in range(lax.axis_size(axis))]
        other = lax.ppermute(gathered, axis, swaps)
        later = (lax.axis_index(axis) & step) != 0
        gathered = jnp.concatenate(
            [jnp.where(later, other, gathered), jnp.where(later, gathered, other)]
        )
    return gathered


def owner_order(part):
    return part.astype(BF16).reshape(8, 2, 8, 8, C).transpose(1, 0, 2, 3, 4)


def reduced(pieces, rows):
    pieces = lax.all_to_all(pieces.reshape(128, rows, C), ("row", "col"), 0, 0, tiled=True)
    return jnp.sum(pieces.astype(F32), axis=0)


def with_halo(cells, sides, width):
    for axis, dim in sides:
        count = lax.axis_size(axis)
        head = lax.slice_in_dim(cells, 0, width, axis=dim).astype(BF16)
        tail_part = lax.slice_in_dim(
            cells, cells.shape[dim] - width, cells.shape[dim], axis=dim
        ).astype(BF16)
        before = lax.ppermute(tail_part, axis, [(i, (i + 1) % count) for i in range(count)])
        after = lax.ppermute(head, axis, [((i + 1) % count, i) for i in range(count)])
        cells = jnp.concatenate(
            [before.astype(cells.dtype), cells, after.astype(cells.dtype)], axis=dim
        )
    return cells


def block(
    field,
    in_weight,
    conv_weight,
    proj_weight,
    dt_weight,
    dt_bias,
    decay_rate,
    skip_gain,
    norm_gain,
    out_weight,
    grad_out,
):
    upper = lax.axis_index("row") >= lax.axis_size("row") // 2
    field_tall = with_halo(field, (("row", 0),), 1)
    in_pieces = sent_to_all(in_weight, "row")
    in_pieces, out_weight = lax.optimization_barrier((in_pieces, out_weight))
    in_source = in_pieces[:8].transpose(1, 0, 2).reshape(C, E)
    in_gate = in_pieces[8:].transpose(1, 0, 2).reshape(C, E)
    out_full = sent_to_all(out_weight, "col").reshape(E, C)
    field_rows = field.reshape(CELLS, C)
    grad_rows = grad_out.reshape(CELLS, C)
    field_wide = with_halo(field_tall, (("col", 1),), 1)
    padded = lax.dot_general(
        field_wide, in_source, (((2,), (0,)), ((), ())), preferred_element_type=F32
    ).astype(BF16)
    gate = jnp.dot(field_rows, in_gate, preferred_element_type=F32).astype(BF16)
    convolved = jnp.zeros((ROWS, COLS, E), F32)
    for a in range(3):
        for b in range(3):
            convolved = (
                convolved + padded[a : a + ROWS, b : b + COLS].astype(F32) * conv_weight[a, b]
            )
    convolved = convolved.reshape(CELLS, E)
    active = jax.nn.silu(convolved).astype(BF16)
    projected = jnp.dot(active, proj_weight, preferred_element_type=F32)

    kinds = ((True, "row", 0), (False, "col", 2))
    width = R + 2 * N
    pads = [
        jnp.stack(
            [
                jnp.pad(dt_weight[k + d], ((d * width, LANES - R - d * width), (0, 0)))
                for d in range(2)
            ]
        )
        for _, _, k in kinds
    ]
    projs = [projected[:, k * width : k * width + LANES] for _, _, k in kinds]
    rates = [decay_rate[k : k + 2] * -LOG2E for _, _, k in kinds]
    skips = [skip_gain[k : k + 1] + skip_gain[k + 1 : k + 2] for _, _, k in kinds]

    sums = [
        block_sums(down, active, projs[i], pads[i], dt_bias[k : k + 2], rates[i])
        for i, (down, _, k) in enumerate(kinds)
    ]
    ends, out_full = lax.optimization_barrier((sums[1][0], out_full))
    sums[1] = (ends, *sums[1][1:])
    back_mixed = lax.dot_general(
        grad_rows, out_full, (((1,), (1,)), ((), ())), preferred_element_type=F32
    )
    infos = [swap(sums[i][0], axis) for i, (_, axis, _) in enumerate(kinds)]
    starts = [
        swap(closed(axis, infos[i], infos[i], rates[i], False), axis)
        for i, (_, axis, _) in enumerate(kinds)
    ]
    outs = [
        block_outputs(down, active, projs[i], sums[i][1], rates[i], skips[i], starts[i])
        for i, (down, _, _) in enumerate(kinds)
    ]
    mixed, back_summed, back_gate = tail(outs[0][0], outs[1][0], gate, norm_gain[None], back_mixed)
    result = (
        field_rows.astype(F32) + jnp.dot(mixed, out_full, preferred_element_type=F32)
    ).astype(BF16)
    out_part = lax.dot_general(
        mixed, grad_rows, (((0,), (0,)), ((), ())), preferred_element_type=F32
    )
    gate_part = lax.dot_general(
        back_gate, field_rows, (((0,), (0,)), ((), ())), preferred_element_type=F32
    )

    back_ends = [
        swap(block_back_sums(down, back_summed, projs[i], sums[i][1], rates[i]), axis)
        for i, (down, axis, _) in enumerate(kinds)
    ]
    pieces = jnp.concatenate(
        [
            out_part.astype(BF16).reshape(8, 16, 8, C).transpose(1, 0, 2, 3).reshape(128, 8, C),
            owner_order(gate_part).reshape(128, 8, C),
        ],
        axis=1,
    )
    out_grads = [
        block_out_grads(down, back_summed, outs[i][1]) for i, (down, _, _) in enumerate(kinds)
    ]
    tails = [
        swap(closed(axis, infos[i], back_ends[i], rates[i], True), axis)
        for i, (_, axis, _) in enumerate(kinds)
    ]
    pieces, tails = lax.optimization_barrier((pieces, tails))
    done_piece = reduced(pieces, 16)
    grads = [
        block_grads(
            down, active, back_summed, projs[i], sums[i][1], sums[i][2], rates[i], skips[i],
            pads[i], outs[i][1], tails[i],
        )
        for i, (down, _, _) in enumerate(kinds)
    ]
    done_piece, grads = lax.optimization_barrier((done_piece, grads))
    grad_out_weight = doubled(done_piece[:8], "row").reshape(E // 8, C)
    gate_piece = done_piece[8:]
    proj_grads = jnp.concatenate([grads[i][1] + out_grads[i] for i in range(2)], axis=1)
    high, low = split(proj_grads)
    dims = (((1,), (1,)), ((), ()))
    back_active = (
        grads[0][0]
        + grads[1][0]
        + lax.dot_general(high, proj_weight, dims, preferred_element_type=F32)
        + lax.dot_general(low, proj_weight, dims, preferred_element_type=F32)
    )
    sig = jax.nn.sigmoid(convolved)
    back_conv = back_active * (sig + convolved * sig * (1.0 - sig))
    wide = with_halo(back_conv.reshape(ROWS, COLS, E), (("row", 0), ("col", 1)), 1)
    back_source = jnp.zeros((ROWS, COLS, E), F32)
    for a in range(3):
        for b in range(3):
            back_source = (
                back_source + wide[2 - a : 2 - a + ROWS, 2 - b : 2 - b + COLS] * conv_weight[a, b]
            )
    back_source = back_source.reshape(CELLS, E).astype(BF16)
    source_part = lax.dot_general(
        back_source, field_rows, (((0,), (0,)), ((), ())), preferred_element_type=F32
    )
    source_piece = reduced(owner_order(source_part).reshape(128, 8, C), 8)
    dims = (((1,), (1,)), ((), ()))
    grad_field = (
        grad_rows.astype(F32)
        + lax.dot_general(back_gate, in_gate, dims, preferred_element_type=F32)
        + lax.dot_general(back_source, in_source, dims, preferred_element_type=F32)
    )
    own = jnp.where(upper, gate_piece, source_piece)
    given = across(jnp.where(upper, source_piece, gate_piece))
    pair = jnp.where(upper, jnp.stack([given, own]), jnp.stack([own, given])).astype(BF16)
    grad_in_weight = (
        sent_to_all(pair, "col").transpose(1, 0, 2, 3).reshape(LANES, C).T.astype(F32)
    )
    return (
        result.reshape(ROWS, COLS, C),
        grad_field.reshape(ROWS, COLS, C),
        grad_in_weight,
        grad_out_weight,
    )


def solution(mesh):
    in_specs = (
        P("row", "col", None),
        P(None, "row"),
        P(),
        P(),
        P(),
        P(),
        P(),
        P(),
        P(),
        P("col", None),
        P("row", "col", None),
    )
    out_specs = (P("row", "col", None), P("row", "col", None), P(None, "row"), P("col", None))
    return jax.shard_map(block, mesh=mesh, in_specs=in_specs, out_specs=out_specs, check_vma=False)
```
